32 devices in a mesh: groups: 2 (over y), tm: 16 (over z, x, core).
Axes of the slice: x: 2, y: 2, z: 4, core: 2. Of those that a mesh axis runs over, the one named last changes fastest.
Arguments:
- noisy: bfloat16 [256, 16, 16, 256], P(('groups', 'tm')), parts along dimension 0, may hold values from -6 to 6
- observed: float32 [256, 16, 256], P(('groups', 'tm')), parts along dimension 0, may hold values from -6 to 6
- obs_mask: int32 [256, 16, 256], P(('groups', 'tm')), parts along dimension 0, may hold values 0 or 1
- obs_channel: int32 [256, 16, 256], P(('groups', 'tm')), parts along dimension 0, may hold values from 0 to 15
- step_index: int32 [2], P('groups'), parts along dimension 0, may hold values from 0 to 63
- w_first: bfloat16 [128, 80, 3, 3], replicated, may hold values from -0.21875 to 0.21875
- b_first: float32 [128], replicated, may hold values from -3 to 3
- w_second: bfloat16 [16, 128, 3, 3], replicated, may hold values from -0.1875 to 0.1875
- b_second: float32 [16], replicated, may hold values from -3 to 3
Outputs:
- guided: float32 [256, 16, 16, 256], P(('groups', 'tm')), parts along dimension 0
The draws below stay inside these ranges and needn't reach their ends.
There are 2 independent parts, one for each index of `groups`. The reference program is written for one: setup_inputs(seed, part) draws one part's arguments, and reference() takes and returns one part's arrays. A program takes and returns all parts, laid end to end along the dimension named above; an argument that names none is the same for every part. Nothing has to cross between parts.
All inputs are finite; a program needn't handle non-finite values. No bound on the sum of `obs_mask` on one device may be relied on, other than what follows from the above.
Results may differ from the reference program's by a relative error of at most 0.0015.
Values may be sent and summed in bfloat16 or wider, within the bound.
No kernel may reach another device: no remote copies, remote signals or barrier semaphores. Data moves between devices by JAX's collectives and lax.ppermute only.
A program may use at most 128 MiB of HBM per device.

```python
import jax
import jax.numpy as jnp
from jax import lax

C = 16
HID = 128
WIN = 5
STEPS = 64
ROWS = 16
COLS = 256
FRAMES = 128


def place_ends(entries, key, least, largest):
    extent = entries.shape
    spot = [jax.random.randint(jax.random.fold_in(key, axis), (), 0, extent[axis]) for axis in range(len(extent))]
    entries = entries.at[tuple(spot)].set(least)
    longest = extent.index(max(extent))
    spot[longest] = (spot[longest] + 1) % extent[longest]
    return entries.at[tuple(spot)].set(largest)


def levels(own_key, dims, shards, least, largest):
    def one(axis_at, blocks):
        draws = jax.random.uniform(jax.random.fold_in(jax.random.fold_in(own_key, 6), axis_at), (blocks,), jnp.float32, least / len(shards), largest / len(shards))
        return jnp.repeat(jnp.exp(draws), dims[axis_at] // blocks).reshape((-1,) + (1,) * (len(dims) - axis_at - 1))

    gain = one(*shards[0])
    for cut in shards[1:]:
        gain = gain * one(*cut)
    return gain


def normal_values(rng, extent, deviation, reach, shards=(), held_as=jnp.bfloat16):
    gain = levels(rng, extent, shards, -0.22, 0.18) if shards else 1.0
    drawn = jax.random.normal(rng, extent, jnp.float32) * deviation * gain
    return jnp.minimum(jnp.maximum(drawn, -reach), reach).astype(held_as)


def setup_inputs(seed: int = 0, part: int = 0) -> dict:
    arg_keys = jax.random.split(jax.random.key(seed), 10)
    part_splits = jax.random.split(jax.random.fold_in(arg_keys[9], part), 10)
    return {
        "noisy": normal_values(part_splits[0], (FRAMES, C, ROWS, COLS), 1.0, 6.0, ((0, 16),)),
        "observed": normal_values(part_splits[1], (FRAMES, ROWS, COLS), 1.0, 6.0, ((0, 16),), jnp.float32),
        "obs_mask": place_ends((jax.random.randint(part_splits[2], (FRAMES, ROWS, COLS), 0, 2) < 1).astype(jnp.int32), jax.random.fold_in(part_splits[2], 1), 0, 1),
        "obs_channel": place_ends(jax.random.randint(part_splits[3], (FRAMES, ROWS, COLS), 0, C), jax.random.fold_in(part_splits[3], 1), 0, C - 1).astype(jnp.int32),
        "step_index": jax.random.randint(part_splits[4], (1,), 0, STEPS).astype(jnp.int32),
        "w_first": normal_values(arg_keys[5], (HID, WIN * C, 3, 3), (9 * WIN * C) ** -0.5, 0.21875),
        "b_first": normal_values(arg_keys[6], (HID,), 0.5, 3.0, (), jnp.float32),
        "w_second": normal_values(arg_keys[7], (C, HID, 3, 3), (9 * HID) ** -0.5, 0.1875),
        "b_second": normal_values(arg_keys[8], (C,), 0.5, 3.0, (), jnp.float32),
    }


sigma_low = 0.1
sigma_ratio = 20.0

def conv(value, kernel):
    return lax.conv_general_dilated(value.astype(jnp.float32), kernel.astype(jnp.float32), (1, 1), ((1, 1), (1, 1)), dimension_numbers=('NCHW', 'OIHW', 'NCHW'), precision=lax.Precision.HIGHEST)

def conv_back(grad, kernel):
    flipped = jnp.transpose(kernel, (1, 0, 2, 3))[:, :, ::-1, ::-1]
    return conv(grad, flipped)

def reference(noisy, observed, obs_mask, obs_channel, step_index, w_first, b_first, w_second, b_second):
    frames = noisy.shape[0]
    chans = noisy.shape[1]
    level = step_index[0].astype(jnp.float32) / jnp.float32(STEPS - 1)
    sigma = jnp.float32(sigma_low) * jnp.exp(jnp.log(jnp.float32(sigma_ratio)) * level)
    c_in = 1.0 / jnp.sqrt(1.0 + sigma * sigma)
    weight_obs = 1.0 / (1.0 + sigma * sigma)
    scaled = (c_in * noisy.astype(jnp.float32)).astype(jnp.bfloat16)
    padded = jnp.pad(scaled, ((2, 2), (0, 0), (0, 0), (0, 0)))
    channel_ids = jnp.arange(chans, dtype=jnp.int32)
    select = ((obs_channel[:, None, :, :] == channel_ids[None, :, None, None]) & (obs_mask[:, None, :, :] == 1)).astype(jnp.float32)
    zero = jnp.int32(0)

    def frame_step(index, carry):
        back_pad, den_all, misfit_all = carry
        tpos = jnp.asarray(index).astype(jnp.int32)
        window = lax.dynamic_slice(padded, (tpos, zero, zero, zero), (WIN, chans, ROWS, COLS)).reshape(1, WIN * chans, ROWS, COLS)
        pre = conv(window, w_first)[0] + b_first[:, None, None]
        hidden = jax.nn.silu(pre).astype(jnp.bfloat16)
        den = noisy[tpos].astype(jnp.float32) + conv(hidden[None], w_second)[0] + b_second[:, None, None]
        misfit = select[tpos] * (den - observed[tpos][None])
        misfit_b = misfit.astype(jnp.bfloat16)
        sig = jax.nn.sigmoid(pre)
        grad_hidden = (conv_back(misfit_b[None], w_second)[0] * (sig * (1.0 + pre * (1.0 - sig)))).astype(jnp.bfloat16)
        grad_window = conv_back(grad_hidden[None], w_first)[0].reshape(WIN, chans, ROWS, COLS)
        old = lax.dynamic_slice(back_pad, (tpos, zero, zero, zero), (WIN, chans, ROWS, COLS))
        back_pad = lax.dynamic_update_slice(back_pad, old + grad_window, (tpos, zero, zero, zero))
        den_all = lax.dynamic_update_slice(den_all, den[None], (tpos, zero, zero, zero))
        misfit_all = lax.dynamic_update_slice(misfit_all, misfit[None], (tpos, zero, zero, zero))
        return (back_pad, den_all, misfit_all)
    start = (jnp.zeros((frames + 4, chans, ROWS, COLS), jnp.float32), jnp.zeros((frames, chans, ROWS, COLS), jnp.float32), jnp.zeros((frames, chans, ROWS, COLS), jnp.float32))
    back_pad, den_all, misfit_all = lax.fori_loop(0, frames, frame_step, start)
    back = back_pad[2:frames + 2]
    return den_all - weight_obs * (misfit_all + c_in * back)
```

```python
import functools

import jax
import jax.numpy as jnp
from jax import lax
from jax.experimental import pallas as pl
from jax.experimental.pallas import tpu as pltpu
from jax.sharding import PartitionSpec as P

STEPS = 64
sigma_low = 0.1
sigma_ratio = 20.0
F32 = jnp.float32
BF16 = jnp.bfloat16


def shifted(x, by):
    lanes = x.shape[1]
    lane = lax.broadcasted_iota(jnp.int32, x.shape, 1)
    edge = 0 if by > 0 else lanes - 1
    return jnp.where(lane == edge, 0.0, pltpu.roll(x, by % lanes, 1))


def main_kernel(
    dims,
    cw,
    b2s,
    noisy,
    before,
    after,
    obs,
    mask,
    chan,
    wf,
    b1,
    ws,
    out,
    sent,
    w1,
    w2t,
    wt1,
    wide,
    nperm,
    deriv,
    part,
    codes,
    mis,
    grads,
    qs,
    rest,
    stage,
):
    frames, chans, rows, cols, hid, span = dims
    half = span // 2
    taps = 9 * chans
    c_in, weight = cw[0], cw[1]
    dot = functools.partial(jnp.dot, preferred_element_type=F32)

    blocks = []
    for k in range(span):
        for ab in range(9):
            blocks.append(wf[ab * span * chans + k * chans : ab * span * chans + (k + 1) * chans, :])
    bias = b1[...]
    high = bias.astype(BF16)
    left = bias - high.astype(F32)
    mid = left.astype(BF16)
    low = (left - mid.astype(F32)).astype(BF16)
    depth = w1.shape[1]
    tail = depth - span * taps
    sub = lax.broadcasted_iota(jnp.int32, (tail, hid), 0)
    extra = jnp.where(
        sub == 0,
        high.astype(F32),
        jnp.where(sub == 1, mid.astype(F32), jnp.where(sub == 2, low.astype(F32), 0.0)),
    )
    blocks.append(extra.astype(BF16))
    stacked = jnp.concatenate(blocks, axis=0).astype(F32) * 0.5
    w1[...] = stacked.T.astype(BF16)
    w2t[...] = (ws[...].astype(F32) * 0.5).T.astype(BF16)
    for sp in range(2):
        for ab in range(9):
            for tp in range(span + 1):
                k = sp - tp + 2 * half
                at = (sp * 9 + ab) * chans
                if 0 <= k < span:
                    piece = wf[ab * span * chans + k * chans : ab * span * chans + (k + 1) * chans, :]
                else:
                    piece = jnp.zeros((chans, hid), BF16)
                wt1[at : at + chans, tp * hid : (tp + 1) * hid] = piece

    row_c = lax.broadcasted_iota(jnp.int32, (chans, cols), 0)
    b2 = jnp.zeros((chans, cols), F32)
    for c in range(chans):
        b2 = jnp.where(row_c == c, b2s[c], b2)

    size = chans * rows
    i0 = lax.broadcasted_iota(jnp.int32, (size, size), 0)
    i1 = lax.broadcasted_iota(jnp.int32, (size, size), 1)
    perm = jnp.where(
        (i0 % chans) * rows + i0 // chans == i1, 1.0, 0.0
    ).astype(BF16)
    zero48 = jnp.zeros((3 * chans, cols), BF16)

    def spread(x, slot):
        scaled = (c_in * x).astype(BF16).astype(F32)
        shifts = [shifted(scaled, 1).astype(BF16), scaled.astype(BF16), shifted(scaled, -1).astype(BF16)]
        wide[slot, 0 : 3 * chans, :] = zero48
        wide[slot, (rows + 1) * 3 * chans :, :] = zero48
        for y in range(rows):
            for b in range(3):
                at = (y + 1) * 3 * chans + b * chans
                wide[slot, at : at + chans, :] = shifts[b][y * chans : (y + 1) * chans, :]

    for f in range(half):
        spread(dot(perm, before[f]), f)
        spread(dot(perm, after[f]), half + frames + f)

    def prepare(f, carry):
        x = dot(perm, noisy[f])
        nperm[f] = x.astype(BF16)
        spread(x, half + f)
        return carry

    lax.fori_loop(0, frames, prepare, 0)

    sub = lax.broadcasted_iota(jnp.int32, (tail, cols), 0)
    ones = jnp.where(sub < 3, 1.0, 0.0).astype(BF16)
    zero_g = jnp.zeros((hid, cols), BF16)
    for f in range(half):
        for y in range(rows):
            grads[f, y] = zero_g
            grads[half + frames + f, y] = zero_g
    mis[0] = zero48
    mis[rows + 1] = zero48

    def forward(f, carry):
        codes[...] = jnp.where(mask[f] == 1, chan[f], -1)

        def hidden_row(r):
            pieces = [wide[f + k, r * 3 * chans : (r + 3) * 3 * chans, :] for k in range(span)]
            h = dot(w1[...], jnp.concatenate(pieces + [ones], axis=0))
            u = 1.0 + jnp.tanh(h)
            act = h * u
            deriv[r] = u * (1.0 + (h + h) - act)
            part[r] = dot(ws[...], act.astype(BF16))

        def misfit_row(y):
            total = None
            for a in range(3):
                r = y + a - 1
                if 0 <= r < rows:
                    term = part[r, a * 3 * chans : (a + 1) * 3 * chans, :]
                    total = term if total is None else total + term
            second = (
                shifted(total[:chans], 1) + total[chans : 2 * chans] + shifted(total[2 * chans :], -1)
            )
            den = nperm[f, y * chans : (y + 1) * chans, :].astype(F32) + second + b2
            code = codes[y : y + 1, :]
            miss = jnp.where(row_c == code, den - obs[f, y : y + 1, :], 0.0)
            rest[f, y * chans : (y + 1) * chans, :] = den - weight * miss
            mis[y + 1, :chans, :] = shifted(miss, -1).astype(BF16)
            mis[y + 1, chans : 2 * chans, :] = miss.astype(BF16)
            mis[y + 1, 2 * chans :, :] = shifted(miss, 1).astype(BF16)

        def grad_row(y):
            v = jnp.concatenate([mis[y + 2], mis[y + 1], mis[y]], axis=0)
            grads[f + half, y] = (dot(w2t[...], v) * deriv[y]).astype(BF16)

        for step in range(rows + 2):
            if step < rows:
                hidden_row(step)
            if 1 <= step <= rows:
                misfit_row(step - 1)
            if step >= 2:
                grad_row(step - 2)
        return carry

    lax.fori_loop(0, frames, forward, 0)

    def put(sp, y, value):
        for j in range(cols // 128):
            stage[sp, j, pl.ds(y, chans, stride=rows), :] = value[:, j * 128 : (j + 1) * 128]

    def back_rows(slots, w, emit):
        def q_row(r):
            v = jnp.concatenate([grads[s, r] for s in slots], axis=0)
            qs[r] = dot(w, v)

        def out_row(y):
            for sp in range(2):
                total = None
                for a in range(3):
                    r = y - a + 1
                    if 0 <= r < rows:
                        at = (sp * 9 + a * 3) * chans
                        term = qs[r, at : at + 3 * chans, :]
                        total = term if total is None else total + term
                back = (
                    shifted(total[:chans], -1)
                    + total[chans : 2 * chans]
                    + shifted(total[2 * chans :], 1)
                )
                emit(sp, y, back)

        for step in range(rows + 1):
            if step < rows:
                q_row(step)
            if step >= 1:
                out_row(step - 1)

    def pair(p, carry):
        s0 = 2 * p

        def emit(sp, y, back):
            own = rest[s0 + sp, y * chans : (y + 1) * chans, :]
            put(sp, y, own - (weight * c_in) * back)

        back_rows([s0 + j for j in range(span + 1)], wt1[...], emit)
        for sp in range(2):
            for j in range(cols // 128):
                out[s0 + sp, :, j * 128 : (j + 1) * 128] = stage[sp, j]
        return carry

    lax.fori_loop(0, frames // 2, pair, 0)

    for side in range(2):
        first = half if side == 0 else frames
        lanes = (span - 1) * hid if side == 0 else 0
        back_rows([first, first + 1], wt1[:, lanes : lanes + 2 * hid], put)
        for sp in range(2):
            for j in range(cols // 128):
                sent[2 * side + sp, :, j * 128 : (j + 1) * 128] = stage[sp, j].astype(BF16)


def per_device(noisy, observed, obs_mask, obs_channel, step_index, w_first, b_first, w_second, b_second):
    frames, chans, rows, cols = noisy.shape
    hid = w_first.shape[0]
    span = w_first.shape[1] // chans
    half = span // 2
    size = chans * rows
    count = lax.axis_size("tm")
    up = [(i, i + 1) for i in range(count - 1)]
    down = [(i + 1, i) for i in range(count - 1)]

    level = step_index[0].astype(F32) / F32(STEPS - 1)
    sigma = F32(sigma_low) * jnp.exp(jnp.log(F32(sigma_ratio)) * level)
    c_in = 1.0 / jnp.sqrt(1.0 + sigma * sigma)
    weight = 1.0 / (1.0 + sigma * sigma)
    cw = jnp.stack([c_in, weight])

    flat = noisy.reshape(frames, size, cols)
    before = lax.ppermute(flat[frames - half :], "tm", up)
    after = lax.ppermute(flat[:half], "tm", down)

    depth = -(-span * 9 * chans // 256) * 256
    dims = (frames, chans, rows, cols, hid, span)
    vmem = pl.BlockSpec(memory_space=pltpu.VMEM)
    smem = pl.BlockSpec(memory_space=pltpu.SMEM)
    out, sent = pl.pallas_call(
        functools.partial(main_kernel, dims),
        out_shape=(
            jax.ShapeDtypeStruct((frames, size, cols), F32),
            jax.ShapeDtypeStruct((2 * half, size, cols), BF16),
        ),
        in_specs=[smem, smem] + [vmem] * 9,
        out_specs=(vmem, vmem),
        scratch_shapes=[
            pltpu.VMEM((hid, depth), BF16),
            pltpu.VMEM((hid, 9 * chans), BF16),
            pltpu.VMEM((18 * chans, (span + 1) * hid), BF16),
            pltpu.VMEM((frames + 2 * half, (rows + 2) * 3 * chans, cols), BF16),
            pltpu.VMEM((frames, size, cols), BF16),
            pltpu.VMEM((rows, hid, cols), F32),
            pltpu.VMEM((rows, 9 * chans, cols), F32),
            pltpu.VMEM((rows, cols), jnp.int32),
            pltpu.VMEM((rows + 2, 3 * chans, cols), BF16),
            pltpu.VMEM((frames + 2 * half, rows, hid, cols), BF16),
            pltpu.VMEM((rows, 18 * chans, cols), F32),
            pltpu.VMEM((frames, size, cols), F32),
            pltpu.VMEM((2, cols // 128, size, 128), F32),
        ],
        compiler_params=pltpu.CompilerParams(vmem_limit_bytes=56 << 20),
    )(
        cw,
        b_second,
        flat,
        before,
        after,
        observed,
        obs_mask,
        obs_channel,
        jnp.transpose(w_first, (2, 3, 1, 0)).reshape(9 * span * chans, hid),
        b_first.reshape(1, hid),
        jnp.transpose(w_second, (2, 3, 0, 1)).reshape(9 * chans, hid),
    )
    from_right = lax.ppermute(sent[:half], "tm", down).astype(F32)
    from_left = lax.ppermute(sent[half:], "tm", up).astype(F32)
    out = out.at[frames - half :].add(-(weight * c_in) * from_right)
    out = out.at[:half].add(-(weight * c_in) * from_left)
    return out.reshape(frames, chans, rows, cols)


def solution(mesh):
    return jax.shard_map(
        per_device,
        mesh=mesh,
        in_specs=(
            P(("groups", "tm"), None, None, None),
            P(("groups", "tm"), None, None),
            P(("groups", "tm"), None, None),
            P(("groups", "tm"), None, None),
            P("groups"),
            P(),
            P(),
            P(),
            P(),
        ),
        out_specs=P(("groups", "tm"), None, None, None),
        check_vma=False,
    )
```

```python
import functools

import jax
import jax.numpy as jnp
from jax import lax
from jax.experimental import pallas as pl
from jax.experimental.pallas import tpu as pltpu
from jax.sharding import PartitionSpec as P

STEPS = 64
sigma_low = 0.1
sigma_ratio = 20.0
F32 = jnp.float32
BF16 = jnp.bfloat16


def shifted(x, by):
    lanes = x.shape[1]
    lane = lax.broadcasted_iota(jnp.int32, x.shape, 1)
    edge = 0 if by > 0 else lanes - 1
    return jnp.where(lane == edge, 0.0, pltpu.roll(x, by % lanes, 1))


class Unit:

    def __init__(self, index):
        self.index = index
        self.turn = 0

    def product(self, sums, left, right):
        slot = self.turn
        self.turn = 1 - slot
        pltpu.matmul_push_rhs(right, slot, self.index)
        at = 0
        for n, total in enumerate(sums):
            size = total.shape[0]
            pltpu.matmul_acc_lhs(
                total, left[at : at + size, :], load_staged_rhs=slot if n == 0 else None
            )
            at += size


def main_kernel(
    dims,
    cw,
    b2s,
    noisy,
    before,
    after,
    obs,
    mask,
    chan,
    wf,
    b1,
    ws,
    out,
    sent,
    w1,
    w2,
    w2t,
    wt1,
    wide,
    nperm,
    deriv,
    part,
    acts,
    mis,
    grads,
    qs,
    rest,
    stage,
):
    frames, chans, rows, cols, hid, span = dims
    half = span // 2
    taps = 9 * chans
    group = 3 * chans
    pairs = rows // 2
    c_in, weight = cw[0], cw[1]
    units = (Unit(0), Unit(1))

    def first_block(k, ab):
        at = (ab * span + k) * chans
        return wf[at : at + chans, :]

    blocks = [first_block(k, ab) for k in range(span) for ab in range(9)]
    bias = b1[...]
    high = bias.astype(BF16)
    left = bias - high.astype(F32)
    mid = left.astype(BF16)
    low = (left - mid.astype(F32)).astype(BF16)
    depth = w1.shape[1]
    tail = depth - span * taps
    sub = lax.broadcasted_iota(jnp.int32, (tail, hid), 0)
    extra = jnp.where(
        sub == 0,
        high.astype(F32),
        jnp.where(sub == 1, mid.astype(F32), jnp.where(sub == 2, low.astype(F32), 0.0)),
    )
    blocks.append(extra.astype(BF16))
    stacked = jnp.concatenate(blocks, axis=0).astype(F32) * 0.5
    w1[...] = stacked.T.astype(BF16)
    second = ws[...]
    zero_group = jnp.zeros((group, hid), BF16)

    def second_block(a):
        return second[a * group : (a + 1) * group, :] if 0 <= a < 3 else zero_group

    for o in range(4):
        for i in range(2):
            w2[o * group : (o + 1) * group, i * hid : (i + 1) * hid] = second_block(i + 2 - o)
    for i in range(2):
        tall = [second_block(i + 2 - m) for m in range(4)]
        tall.append(jnp.zeros((2 * hid - 4 * group, hid), BF16))
        tall = jnp.concatenate(tall, axis=0).astype(F32) * 0.5
        w2t[i * hid : (i + 1) * hid, :] = tall.T.astype(BF16)
    for sp in range(2):
        for ab in range(9):
            for tp in range(span + 1):
                k = sp - tp + 2 * half
                at = (sp * 9 + ab) * chans
                piece = first_block(k, ab) if 0 <= k < span else jnp.zeros((chans, hid), BF16)
                wt1[at : at + chans, tp * hid : (tp + 1) * hid] = piece

    row_c = lax.broadcasted_iota(jnp.int32, (chans, cols), 0)
    b2 = jnp.zeros((chans, cols), F32)
    for c in range(chans):
        b2 = jnp.where(row_c == c, b2s[c], b2)

    size = chans * rows
    i0 = lax.broadcasted_iota(jnp.int32, (size, size), 0)
    i1 = lax.broadcasted_iota(jnp.int32, (size, size), 1)
    perm = jnp.where((i0 % chans) * rows + i0 // chans == i1, 1.0, 0.0).astype(BF16)
    zero48 = jnp.zeros((group, cols), BF16)

    def spread(x, slot, y0):
        scaled = (c_in * x).astype(BF16).astype(F32)
        shifts = [shifted(scaled, 1).astype(BF16), scaled.astype(BF16), shifted(scaled, -1).astype(BF16)]
        for y in range(x.shape[0] // chans):
            for b in range(3):
                at = (y0 + y + 1) * group + b * chans
                wide[slot, at : at + chans, :] = shifts[b][y * chans : (y + 1) * chans, :]

    def reorder(totals):
        def frame(m, source, slot, own):
            units[m].product(totals[m], perm, source)
            wide[slot, 0:group, :] = zero48
            wide[slot, (rows + 1) * group :, :] = zero48

        def finish(m, slot, own):
            at = 0
            for total in totals[m]:
                x = matmul_pop(total)
                if own is not None:
                    nperm[own, at : at + x.shape[0], :] = x.astype(BF16)
                spread(x, slot, at // chans)
                at += x.shape[0]

        for f in range(half):
            frame(0, before[f], f, None)
            frame(1, after[f], half + frames + f, None)
            finish(0, f, None)
            finish(1, half + frames + f, None)

        def prepare(p, carry):
            for m in range(2):
                frame(m, noisy[2 * p + m], half + 2 * p + m, 2 * p + m)
            for m in range(2):
                finish(m, half + 2 * p + m, 2 * p + m)
            return carry

        lax.fori_loop(0, frames // 2, prepare, 0)

    matmul_pop = pltpu.matmul_pop
    pl.run_scoped(reorder, [[pltpu.ACC(m)((size // 4, cols), F32) for _ in range(4)] for m in range(2)])

    sub = lax.broadcasted_iota(jnp.int32, (tail, cols), 0)
    ones = jnp.where(sub < 3, 1.0, 0.0).astype(BF16)
    zero_g = jnp.zeros((hid, cols), BF16)
    for f in range(half):
        for y in range(rows):
            grads[f, y] = zero_g
            grads[half + frames + f, y] = zero_g
    mis[...] = jnp.zeros(mis.shape, BF16)

    def forward(sums1, sums2, sums3):

        def issue_first(f, t):
            for m in range(2):
                r = 2 * t + m
                pieces = [wide[f + k, r * group : (r + 3) * group, :] for k in range(span)]
                v = jnp.concatenate(pieces + [ones], axis=0)
                for k in range(depth // cols):
                    units[m].product(
                        sums1[m][t % 2], w1.at[:, k * 256 : (k + 1) * 256], v[k * 256 : (k + 1) * 256, :]
                    )

        def activate(f, t):
            for m in range(2):
                at = 0
                for total in sums1[m][t % 2]:
                    h = pltpu.matmul_pop(total)
                    u = 1.0 + jnp.tanh(h)
                    act = h * u
                    deriv[f % 2, 2 * t + m, at : at + h.shape[0], :] = u * (1.0 + (h + h) - act)
                    acts[t % 2, m * hid + at : m * hid + at + h.shape[0], :] = act.astype(BF16)
                    at += h.shape[0]

        def issue_second(t):
            units[0].product(sums2[t % 2], w2, acts[t % 2])

        def keep_second(f, t):
            for o in range(4):
                part[f % 2, t, o * group : (o + 1) * group, :] = pltpu.matmul_pop(sums2[t % 2][o])

        def misfit_row(g, y):
            t, i = y // 2, y % 2
            total = part[g % 2, t, (1 + i) * group : (2 + i) * group, :]
            other, o = (t + 1, 0) if i else (t - 1, 3)
            if 0 <= other < pairs:
                total = total + part[g % 2, other, o * group : (o + 1) * group, :]
            conv = shifted(total[:chans], 1) + total[chans : 2 * chans] + shifted(total[2 * chans :], -1)
            den = nperm[g, y * chans : (y + 1) * chans, :].astype(F32) + conv + b2
            seen = mask[g, y : y + 1, :]
            code = jnp.where(seen == 1, chan[g, y : y + 1, :], -1)
            miss = jnp.where(row_c == code, den - obs[g, y : y + 1, :], 0.0)
            rest[g, y * chans : (y + 1) * chans, :] = den - weight * miss
            at = (y + 1) * group
            mis[at : at + chans, :] = shifted(miss, -1).astype(BF16)
            mis[at + chans : at + 2 * chans, :] = miss.astype(BF16)
            mis[at + 2 * chans : at + 3 * chans, :] = shifted(miss, 1).astype(BF16)

        def issue_third(q):
            at = 2 * q * group
            units[1].product(sums3[q % 2], w2t, mis[at : at + 2 * hid, :])

        def keep_third(g, q):
            at = 0
            for total in sums3[q % 2]:
                n = total.shape[0]
                i, low = at // hid, at % hid
                y = 2 * q + i
                d = pltpu.matmul_pop(total) * deriv[g % 2, y, low : low + n, :]
                grads[g + half, y, low : low + n, :] = d.astype(BF16)
                at += n

        def body(f, g):
            for t in range(pairs + 3):
                if f is not None and 2 <= t < pairs + 2:
                    issue_second(t - 2)
                if g is not None and 2 <= t < pairs + 2:
                    issue_third(t - 2)
                if f is not None and t < pairs:
                    issue_first(f, t)
                if f is not None and 1 <= t < pairs + 1:
                    activate(f, t - 1)
                if g is not None:
                    for y in (2 * t, 2 * t + 1):
                        if y < rows:
                            misfit_row(g, y)
                if f is not None and 3 <= t < pairs + 3:
                    keep_second(f, t - 3)
                if g is not None and 3 <= t < pairs + 3:
                    keep_third(g, t - 3)

        body(0, None)

        def step(f, carry):
            body(f, f - 1)
            return carry

        lax.fori_loop(1, frames, step, 0)
        body(None, frames - 1)

    def sums(unit, size, n):
        return [[pltpu.ACC(unit)((size, cols), F32) for _ in range(n)] for _ in range(2)]

    pl.run_scoped(
        forward,
        [sums(m, hid // 2, 2) for m in range(2)],
        sums(0, group, 4),
        sums(1, hid // 2, 4),
    )

    def put(sp, y, value):
        for j in range(cols // 128):
            stage[sp, j, pl.ds(y, chans, stride=rows), :] = value[:, j * 128 : (j + 1) * 128]

    def back_rows(totals, slots, w, emit):
        def issue(t):
            for m in range(2):
                r = 2 * t + m
                for k in range(len(slots) // 2):
                    v = jnp.concatenate([grads[slots[2 * k], r], grads[slots[2 * k + 1], r]], axis=0)
                    units[m].product(totals[m][t % 2], w.at[:, k * 256 : (k + 1) * 256], v)

        def keep(t):
            for m in range(2):
                at = 0
                for total in totals[m][t % 2]:
                    n = total.shape[0]
                    qs[2 * t + m, at : at + n, :] = pltpu.matmul_pop(total)
                    at += n

        def out_row(y):
            for sp in range(2):
                total = None
                for a in range(3):
                    r = y - a + 1
                    if 0 <= r < rows:
                        at = (sp * 3 + a) * group
                        term = qs[r, at : at + group, :]
                        total = term if total is None else total + term
                back = (
                    shifted(total[:chans], -1)
                    + total[chans : 2 * chans]
                    + shifted(total[2 * chans :], 1)
                )
                emit(sp, y, back)

        for t in range(pairs + 2):
            if t < pairs:
                issue(t)
            if 1 <= t < pairs + 1:
                keep(t - 1)
            for y in (2 * t - 5, 2 * t - 4):
                if 0 <= y < rows:
                    out_row(y)
        out_row(rows - 1)

    def backward(totals):
        def pair(p, carry):
            s0 = 2 * p

            def emit(sp, y, back):
                own = rest[s0 + sp, y * chans : (y + 1) * chans, :]
                put(sp, y, own - (weight * c_in) * back)

            back_rows(totals, [s0 + j for j in range(span + 1)], wt1, emit)
            for sp in range(2):
                for j in range(cols // 128):
                    out[s0 + sp, :, j * 128 : (j + 1) * 128] = stage[sp, j]
            return carry

        lax.fori_loop(0, frames // 2, pair, 0)

        for side in range(2):
            first = half if side == 0 else frames
            lanes = (span - 1) * hid if side == 0 else 0
            back_rows(totals, [first, first + 1], wt1.at[:, lanes : lanes + 2 * hid], put)
            for sp in range(2):
                for j in range(cols // 128):
                    sent[2 * side + sp, :, j * 128 : (j + 1) * 128] = stage[sp, j].astype(BF16)

    pl.run_scoped(backward, [sums(m, 2 * group, 3) for m in range(2)])


def local(cw, b2s, noisy, before, after, observed, obs_mask, obs_channel, wf, b1, ws):
    frames, size, cols = noisy.shape
    rows = observed.shape[1]
    chans = size // rows
    hid = wf.shape[1]
    span = wf.shape[0] // (9 * chans)
    half = span // 2
    depth = -(-span * 9 * chans // 256) * 256
    dims = (frames, chans, rows, cols, hid, span)
    vmem = pl.BlockSpec(memory_space=pltpu.VMEM)
    smem = pl.BlockSpec(memory_space=pltpu.SMEM)
    return pl.pallas_call(
        functools.partial(main_kernel, dims),
        out_shape=(
            jax.ShapeDtypeStruct((frames, size, cols), F32),
            jax.ShapeDtypeStruct((2 * half, size, cols), BF16),
        ),
        in_specs=[smem, smem] + [vmem] * 9,
        out_specs=(vmem, vmem),
        scratch_shapes=[
            pltpu.VMEM((hid, depth), BF16),
            pltpu.VMEM((12 * chans, 2 * hid), BF16),
            pltpu.VMEM((2 * hid, 2 * hid), BF16),
            pltpu.VMEM((18 * chans, (span + 1) * hid), BF16),
            pltpu.VMEM((frames + 2 * half, (rows + 2) * 3 * chans, cols), BF16),
            pltpu.VMEM((frames, size, cols), BF16),
            pltpu.VMEM((2, rows, hid, cols), F32),
            pltpu.VMEM((2, rows // 2, 12 * chans, cols), F32),
            pltpu.VMEM((2, 2 * hid, cols), BF16),
            pltpu.VMEM(((rows + 2) * 3 * chans + 2 * hid, cols), BF16),
            pltpu.VMEM((frames + 2 * half, rows, hid, cols), BF16),
            pltpu.VMEM((rows, 18 * chans, cols), F32),
            pltpu.VMEM((frames, size, cols), F32),
            pltpu.VMEM((2, cols // 128, size, 128), F32),
        ],
        compiler_params=pltpu.CompilerParams(vmem_limit_bytes=56 << 20),
    )(cw, b2s, noisy, before, after, observed, obs_mask, obs_channel, wf, b1, ws)


def per_device(noisy, observed, obs_mask, obs_channel, step_index, w_first, b_first, w_second, b_second):
    frames, chans, rows, cols = noisy.shape
    hid = w_first.shape[0]
    span = w_first.shape[1] // chans
    half = span // 2
    size = chans * rows
    count = lax.axis_size("tm")
    up = [(i, i + 1) for i in range(count - 1)]
    down = [(i + 1, i) for i in range(count - 1)]

    level = step_index[0].astype(F32) / F32(STEPS - 1)
    sigma = F32(sigma_low) * jnp.exp(jnp.log(F32(sigma_ratio)) * level)
    c_in = 1.0 / jnp.sqrt(1.0 + sigma * sigma)
    weight = 1.0 / (1.0 + sigma * sigma)
    cw = jnp.stack([c_in, weight])

    flat = noisy.reshape(frames, size, cols)
    before = lax.ppermute(flat[frames - half :], "tm", up)
    after = lax.ppermute(flat[:half], "tm", down)

    out, sent = local(
        cw,
        b_second,
        flat,
        before,
        after,
        observed,
        obs_mask,
        obs_channel,
        jnp.transpose(w_first, (2, 3, 1, 0)).reshape(9 * span * chans, hid),
        b_first.reshape(1, hid),
        jnp.transpose(w_second, (2, 3, 0, 1)).reshape(9 * chans, hid),
    )
    from_right = lax.ppermute(sent[:half], "tm", down).astype(F32)
    from_left = lax.ppermute(sent[half:], "tm", up).astype(F32)
    out = out.at[frames - half :].add(-(weight * c_in) * from_right)
    out = out.at[:half].add(-(weight * c_in) * from_left)
    return out.reshape(frames, chans, rows, cols)


def solution(mesh):
    return jax.shard_map(
        per_device,
        mesh=mesh,
        in_specs=(
            P(("groups", "tm"), None, None, None),
            P(("groups", "tm"), None, None),
            P(("groups", "tm"), None, None),
            P(("groups", "tm"), None, None),
            P("groups"),
            P(),
            P(),
            P(),
            P(),
        ),
        out_specs=P(("groups", "tm"), None, None, None),
        check_vma=False,
    )
```

```python
import functools

import jax
import jax.numpy as jnp
import numpy as np
from jax import lax
from jax.experimental import pallas as pl
from jax.experimental.pallas import tpu as pltpu
from jax.sharding import PartitionSpec as P

STEPS = 64
sigma_low = 0.1
sigma_ratio = 20.0
F32 = jnp.float32
BF16 = jnp.bfloat16
CHUNK = 32


def shifted(x, by):
    lanes = x.shape[1]
    lane = lax.broadcasted_iota(jnp.int32, x.shape, 1)
    edge = 0 if by > 0 else lanes - 1
    return jnp.where(lane == edge, 0.0, pltpu.roll(x, by % lanes, 1))


def sums_for(unit, size, cols, n, copies=2):
    return [[pltpu.ACC(unit)((size, cols), F32) for _ in range(n)] for _ in range(copies)]


def level_rows(step, cols):
    level = jnp.full((1, cols), step, jnp.int32).astype(F32) / F32(STEPS - 1)
    sigma = F32(sigma_low) * jnp.exp(F32(np.log(sigma_ratio)) * level)
    square = 1.0 + sigma * sigma
    return 1.0 / jnp.sqrt(square), 1.0 / square


class Copy:

    def __init__(self, make):
        self.make = make

    def start(self):
        self.make().start()

    def wait(self):
        self.make().wait()


class Unit:

    def __init__(self, index):
        self.index = index
        self.turn = 0

    def steps(self, sums, left, right):
        slot = self.turn
        self.turn = 1 - slot
        work = [lambda: pltpu.matmul_push_rhs(right(), slot, self.index)]
        at = 0
        for n, total in enumerate(sums):
            size = total.shape[0]

            def add(total=total, at=at, size=size, first=n == 0):
                pltpu.matmul_acc_lhs(
                    total, left[at : at + size, :], load_staged_rhs=slot if first else None
                )

            work.append(add)
            at += size
        return work

    def product(self, sums, left, right):
        for piece in self.steps(sums, left, lambda: right):
            piece()


def weave(*lists):
    keyed = []
    for which, pieces in enumerate(lists):
        for n, piece in enumerate(pieces):
            keyed.append(((n + 0.5) / len(pieces), which, n, piece))
    for entry in sorted(keyed, key=lambda e: e[:3]):
        entry[3]()


def build_weights(dims, wf, b1, ws, w1, w2, w2t, wt1):
    frames, chans, rows, cols, hid, span = dims
    half = span // 2
    taps = 9 * chans
    group = 3 * chans

    def first_block(k, ab):
        at = (ab * span + k) * chans
        return wf[at : at + chans, :]

    blocks = [first_block(k, ab) for k in range(span) for ab in range(9)]
    bias = b1[...]
    high = bias.astype(BF16)
    left = bias - high.astype(F32)
    mid = left.astype(BF16)
    low = (left - mid.astype(F32)).astype(BF16)
    depth = w1.shape[1]
    tail = depth - span * taps
    sub = lax.broadcasted_iota(jnp.int32, (tail, hid), 0)
    extra = jnp.where(
        sub == 0,
        high.astype(F32),
        jnp.where(sub == 1, mid.astype(F32), jnp.where(sub == 2, low.astype(F32), 0.0)),
    )
    blocks.append(extra.astype(BF16))
    stacked = jnp.concatenate(blocks, axis=0).astype(F32) * 0.5
    w1[...] = stacked.T.astype(BF16)
    second = ws[...]
    zero_group = jnp.zeros((group, hid), BF16)

    def second_block(a):
        return second[a * group : (a + 1) * group, :] if 0 <= a < 3 else zero_group

    for o in range(4):
        for i in range(2):
            w2[o * group : (o + 1) * group, i * hid : (i + 1) * hid] = second_block(i + 2 - o)
    for i in range(2):
        tall = [second_block(i + 2 - m) for m in range(4)]
        tall.append(jnp.zeros((2 * hid - 4 * group, hid), BF16))
        tall = jnp.concatenate(tall, axis=0).astype(F32) * 0.5
        w2t[i * hid : (i + 1) * hid, :] = tall.T.astype(BF16)
    for sp in range(2):
        for ab in range(9):
            for tp in range(span + 1):
                k = sp - tp + 2 * half
                at = (sp * 9 + ab) * chans
                piece = first_block(k, ab) if 0 <= k < span else jnp.zeros((chans, hid), BF16)
                wt1[at : at + chans, tp * hid : (tp + 1) * hid] = piece


def reorder_frames(dims, units, c_in, perm, wide, jobs, loops):
    frames, chans, rows, cols, hid, span = dims
    group = 3 * chans
    size = chans * rows
    i0 = lax.broadcasted_iota(jnp.int32, (size, size), 0)
    i1 = lax.broadcasted_iota(jnp.int32, (size, size), 1)
    perm[...] = jnp.where((i0 % chans) * rows + i0 // chans == i1, 1.0, 0.0).astype(BF16)
    zero = jnp.zeros((group, cols), BF16)

    def spread(x, slot, y0):
        scaled = (c_in * x).astype(BF16).astype(F32)
        shifts = [shifted(scaled, 1).astype(BF16), scaled.astype(BF16), shifted(scaled, -1).astype(BF16)]
        for y in range(x.shape[0] // chans):
            for b in range(3):
                at = (y0 + y + 1) * group + b * chans
                wide[slot, at : at + chans, :] = shifts[b][y * chans : (y + 1) * chans, :]

    def run(totals):
        def step(j, carry):
            for m in range(2):
                source, slot, keep = jobs(j, m)
                units[m].product(totals[m], perm, source())
                wide[slot, 0:group, :] = zero
                wide[slot, (rows + 1) * group :, :] = zero
            for m in range(2):
                source, slot, keep = jobs(j, m)
                at = 0
                for total in totals[m]:
                    x = pltpu.matmul_pop(total)
                    keep(at, x)
                    spread(x, slot, at // chans)
                    at += x.shape[0]
            return carry

        lax.fori_loop(0, loops, step, 0)

    pl.run_scoped(run, [sums_for(m, size // 4, cols, 4, 1)[0] for m in range(2)])


def forward_frames(
    dims, units, weight, b2s, w1, w2, w2t, wide, nperm, obs, mask, chan, deriv, part, acts, mis, grads, rest, count, where,
    need, done, noisy0,
):
    frames, chans, rows, cols, hid, span = dims
    group = 3 * chans
    pairs = rows // 2
    depth = w1.shape[1]
    tail = depth - span * 9 * chans
    sub = lax.broadcasted_iota(jnp.int32, (tail, cols), 0)
    ones = jnp.where(sub < 3, 1.0, 0.0).astype(BF16)
    row_c = lax.broadcasted_iota(jnp.int32, (chans, cols), 0)
    b2 = jnp.zeros((chans, cols), F32)
    for c in range(chans):
        b2 = jnp.where(row_c == c, b2s[c], b2)
    mis[...] = jnp.zeros(mis.shape, BF16)

    def forward(sums1, sums2, sums3):

        def issue_first(f, t):
            work = []
            for k in range(depth // cols):
                for m in range(2):
                    r = 2 * t + m

                    def right(k=k, r=r):
                        pieces = [wide[where(f)[1] + b, r * group : (r + 3) * group, :] for b in range(span)]
                        v = jnp.concatenate(pieces + [ones], axis=0)
                        return v[k * 256 : (k + 1) * 256, :]

                    work.append(units[m].steps(sums1[m][t % 2], w1.at[:, k * 256 : (k + 1) * 256], right))
            return [piece for a, b in zip(work[0::2], work[1::2]) for both in zip(a, b) for piece in both]

        def activate(t, save):
            work = []
            for m in range(2):
                at = 0
                for total in sums1[m][t % 2]:

                    def piece(m=m, at=at, total=total):
                        h = pltpu.matmul_pop(total)
                        u = 1.0 + jnp.tanh(h)
                        act = h * u
                        deriv[save][2 * t + m, at : at + h.shape[0], :] = u * (1.0 + (h + h) - act)
                        acts[t % 2, m * hid + at : m * hid + at + h.shape[0], :] = act.astype(BF16)

                    work.append(piece)
                    at += total.shape[0]
            return work

        def issue_second(t):
            return units[0].steps(sums2[t % 2], w2, lambda: acts[t % 2])

        def keep_second(t, save):
            def piece(o):
                part[save][t, o * group : (o + 1) * group, :] = pltpu.matmul_pop(sums2[t % 2][o])

            return [functools.partial(piece, o) for o in range(4)]

        def misfit_row(g, y, load):
            t, i = y // 2, y % 2
            total = part[load][t, (1 + i) * group : (2 + i) * group, :]
            other, o = (t + 1, 0) if i else (t - 1, 3)
            if 0 <= other < pairs:
                total = total + part[load][other, o * group : (o + 1) * group, :]
            conv = shifted(total[:chans], 1) + total[chans : 2 * chans] + shifted(total[2 * chans :], -1)
            den = nperm[noisy0 + where(g)[0], y * chans : (y + 1) * chans, :].astype(F32) + conv + b2
            seen = mask[where(g)[0], y : y + 1, :]
            code = jnp.where(seen == 1, chan[where(g)[0], y : y + 1, :], -1)
            miss = jnp.where(row_c == code, den - obs[where(g)[0], y : y + 1, :], 0.0)
            rest[where(g)[3], y * chans : (y + 1) * chans, :] = den - weight * miss
            at = (y + 1) * group
            mis[g % 2, at : at + chans, :] = shifted(miss, -1).astype(BF16)
            mis[g % 2, at + chans : at + 2 * chans, :] = miss.astype(BF16)
            mis[g % 2, at + 2 * chans : at + 3 * chans, :] = shifted(miss, 1).astype(BF16)

        def issue_third(g, q):
            at = 2 * q * group
            return units[1].steps(sums3[q % 2], w2t, lambda: mis[g % 2, at : at + 2 * hid, :])

        def keep_third(g, q, load):
            work = []
            at = 0
            for total in sums3[q % 2]:

                def piece(at=at, total=total):
                    n = total.shape[0]
                    i, low = at // hid, at % hid
                    y = 2 * q + i
                    d = pltpu.matmul_pop(total) * deriv[load][y, low : low + n, :]
                    grads[where(g)[2], y, low : low + n, :] = d.astype(BF16)

                work.append(piece)
                at += total.shape[0]
            return work

        total = count * pairs
        lag = 6
        for n in range(total + lag + 2):
            first, small, vector = [], [], []
            if 2 <= n < total + 2:
                small += issue_second((n - 2) % pairs)
            q = n - lag - 1
            if 0 <= q < total:
                small += issue_third(q // pairs, q % pairs)
            if n < total:
                if n % pairs == 0:
                    need(n // pairs)
                first += issue_first(n // pairs, n % pairs)
            if 1 <= n < total + 1:
                vector.append(activate((n - 1) % pairs, (n - 1) // pairs % 2))
            if 3 <= n < total + 3:
                vector.append(keep_second((n - 3) % pairs, (n - 3) // pairs % 2))
            q = n - lag + 1
            if 0 <= q < total:
                g, t = q // pairs, q % pairs
                ys = ([2 * t - 1] if t else []) + [2 * t] + ([rows - 1] if t == pairs - 1 else [])
                vector.append([functools.partial(misfit_row, g, y, g % 2) for y in ys])
            q = n - lag - 2
            if q >= 0:
                vector.append(keep_third(q // pairs, q % pairs, q // pairs % 2))
            weave(small + first, *vector)
            if q >= 0 and q % pairs == pairs - 1:
                done(q // pairs)

    pl.run_scoped(
        forward,
        [sums_for(m, CHUNK, cols, hid // CHUNK) for m in range(2)],
        sums_for(0, group, cols, 4),
        sums_for(1, CHUNK, cols, 2 * hid // CHUNK),
    )


def backward_frames(dims, units, scale, wt1, grads, qs, rest, stage, out, first, done):
    frames, chans, rows, cols, hid, span = dims
    group = 3 * chans
    pairs = rows // 2

    def put(p, sp, y, value):
        for j in range(cols // 128):
            stage[p % 2, sp, j, pl.ds(y, chans, stride=rows), :] = value[:, j * 128 : (j + 1) * 128]

    def issue(totals, p, t):
        work = []
        for k in range((span + 1) // 2):
            for m in range(2):

                def right(r=2 * t + m, slot=2 * p + 2 * k):
                    return jnp.concatenate([grads[slot, r], grads[slot + 1, r]], axis=0)

                work.append(units[m].steps(totals[m][t % 2], wt1.at[:, k * 256 : (k + 1) * 256], right))
        return [piece for a, b in zip(work[0::2], work[1::2]) for both in zip(a, b) for piece in both]

    def keep(totals, p, t):
        work = []
        for m in range(2):
            at = 0
            for total in totals[m][t % 2]:

                def piece(m=m, at=at, total=total):
                    qs[p % 2, 2 * t + m, at : at + total.shape[0], :] = pltpu.matmul_pop(total)

                work.append(piece)
                at += total.shape[0]
        return work

    def out_row(p, y, sp):
        total = None
        for a in range(3):
            r = y - a + 1
            if 0 <= r < rows:
                at = (sp * 3 + a) * group
                term = qs[p % 2, r, at : at + group, :]
                total = term if total is None else total + term
        back = shifted(total[:chans], -1) + total[chans : 2 * chans] + shifted(total[2 * chans :], 1)
        own = rest[first + 2 * p + sp, y * chans : (y + 1) * chans, :]
        put(p, sp, y, own - scale * back)

    def store(p):
        for sp in range(2):
            for j in range(cols // 128):
                out[2 * p + sp, :, j * 128 : (j + 1) * 128] = stage[p % 2, sp, j]

    def backward(totals):
        steps = frames // 2 * pairs
        for n in range(steps + 2):
            lists = []
            if n < steps:
                lists.append(issue(totals, n // pairs, n % pairs))
            q = n - 1
            if 0 <= q < steps:
                lists.append(keep(totals, q // pairs, q % pairs))
            q = n - 2
            if q >= 0:
                p, t = q // pairs, q % pairs
                ys = ([2 * t - 1] if t else []) + [2 * t] + ([rows - 1] if t == pairs - 1 else [])
                lists.append([functools.partial(out_row, p, y, sp) for y in ys for sp in range(2)])
            weave(*lists)
            if q >= 0 and t == pairs - 1:
                store(p)
                done(p)

    pl.run_scoped(backward, [sums_for(m, group, cols, 6) for m in range(2)])


def pack_kernel(dims, noisy, obs, mask, chan, up, down, planes, obs_s, mask_s, chan_s, sems):
    frames, chans, rows, cols, hid, span = dims
    half = span // 2
    size = chans * rows
    own = 2 * half
    ends = ((up, frames - own, frames - half), (down, 0, 0))
    copies = []

    def copy(src, dst, n):
        copies.append(pltpu.make_async_copy(src, dst, sems.at[n]))
        copies[-1].start()

    for d, (to, first, frame0) in enumerate(ends):
        for n, (src, dst) in enumerate(((obs, obs_s), (mask, mask_s), (chan, chan_s))):
            copy(src.at[pl.ds(frame0, half)], dst.at[d], 4 * d + n)
    for d, (to, first, frame0) in enumerate(ends):
        for n in range(own):
            copy(noisy.at[first + n], planes.at[d, pl.ds(n * size, size)], 8 + own * d + n)
    for c in copies[:6]:
        c.wait()
    for d in range(2):
        at = own * size
        for n in range(half):
            seen = mask_s[d, n].astype(F32).astype(BF16)
            which = chan_s[d, n].astype(F32).astype(BF16)
            value = obs_s[d, n]
            high = value.astype(BF16)
            left = value - high.astype(F32)
            mid = left.astype(BF16)
            low = (left - mid.astype(F32)).astype(BF16)
            for plane in (seen, which, high, mid, low):
                planes[d, at : at + rows, :] = plane
                at += rows
    for d in range(2):
        for c in copies[6 + own * d : 6 + own * (d + 1)]:
            c.wait()
        copy(planes.at[d], ends[d][0], 4 * d + 3)
    for c in copies[-2:]:
        c.wait()


def inner_kernel(
    dims, step, b2s, noisy, obs, mask, chan, wf, b1, ws,
    wide_out, nperm_out, grads_out, rest_out, w1_out, w2_out, w2t_out, wt1_out,
    w1, w2, w2t, wt1, perm, wide, nperm, noisy_s, obs_s, mask_s, chan_s, deriv0, deriv1, part0, part1, acts, mis,
    grads, rest, sems,
):
    frames, chans, rows, cols, hid, span = dims
    half = span // 2
    inner = frames - 2 * half
    units = (Unit(0), Unit(1))
    c_in, weight = level_rows(step[0], cols)
    arriving = [
        Copy(
            lambda n=n: pltpu.make_async_copy(
                noisy.at[pl.ds(2 * n, 2)], noisy_s.at[pl.ds(2 * n, 2)], sems.at[n]
            )
        )
        for n in range(frames // 2)
    ]
    for a, b in ((obs, obs_s), (mask, mask_s), (chan, chan_s)):
        at = len(arriving)
        arriving.append(
            Copy(lambda a=a, b=b, at=at: pltpu.make_async_copy(a.at[pl.ds(half, inner)], b, sems.at[at]))
        )
    for c in arriving:
        c.start()
    copies = []

    def leave(a, b, i=None):
        at = len(arriving) + len(copies)

        def make():
            if i is None:
                return pltpu.make_async_copy(a, b, sems.at[at])
            return pltpu.make_async_copy(a.at[i], b.at[i], sems.at[at])

        copies.append(Copy(make))
        copies[-1].start()

    build_weights(dims, wf, b1, ws, w1, w2, w2t, wt1)
    for a, b in ((w1, w1_out), (w2, w2_out), (w2t, w2t_out), (wt1, wt1_out)):
        leave(a, b)

    def jobs(j, m):
        f = 2 * j + m

        def keep(at, x):
            nperm[f, at : at + x.shape[0], :] = x.astype(BF16)

        return (lambda: noisy_s[f]), f, keep

    for c in arriving[: frames // 2]:
        c.wait()
    reorder_frames(dims, units, c_in, perm, wide, jobs, frames // 2)
    leave(wide, wide_out)
    leave(nperm, nperm_out)
    for c in arriving[frames // 2 :]:
        c.wait()

    def done(i):
        leave(grads, grads_out, i)
        leave(rest, rest_out, i)

    forward_frames(
        dims, units, weight, b2s, w1, w2, w2t, wide, nperm, obs_s, mask_s, chan_s, (deriv0, deriv1), (part0, part1),
        acts, mis, grads, rest, inner, lambda i: (i, i, i, i), lambda i: None, done, half,
    )
    for copy in copies:
        copy.wait()


def outer_kernel(
    dims, step, b2s, obs, mask, chan, before, after,
    wide_in, nperm_in, grads_in, rest_in, w1_in, w2_in, w2t_in, wt1_in,
    out,
    w1, w2, w2t, wt1, perm, wide, nperm, before_s, after_s, seen, which, value, deriv0, deriv1, part0, part1, acts, mis,
    grads, rest, qs, stage, result, sems,
):
    frames, chans, rows, cols, hid, span = dims
    half = span // 2
    size = chans * rows
    own = 2 * half
    units = (Unit(0), Unit(1))
    inner = frames - 2 * half
    c_in, weight = level_rows(step[0], cols)
    copies = []

    def arrive(a, b, from_at=None, to_at=None, count=None):
        n = len(copies)

        def make():
            src = a if from_at is None else a.at[pl.ds(from_at, count)]
            dst = b if to_at is None else b.at[pl.ds(to_at, count)]
            return pltpu.make_async_copy(src, dst, sems.at[n])

        copies.append(Copy(make))
        copies[-1].start()

    arrive(before, before_s)
    arrive(after, after_s)
    for a, b in ((mask, seen), (chan, which), (obs, value)):
        arrive(a, b, 0, half, half)
        arrive(a, b, frames - half, 2 * half, half)
    for a, b in ((w1_in, w1), (w2_in, w2), (w2t_in, w2t)):
        arrive(a, b)
    arrive(nperm_in, nperm, 0, half, half)
    arrive(nperm_in, nperm, frames - half, 2 * half, half)
    early = len(copies)
    for n in range(frames):
        arrive(wide_in, wide, n, own + n, 1)
    wides = len(copies)
    arrive(wt1_in, wt1)
    arrive(grads_in, grads, 0, 2 * half, inner)
    arrive(rest_in, rest, 0, 2 * half, inner)

    def jobs(j, m):
        src = after_s if m else before_s
        slot = own + frames + j if m else j
        keeps = j < half if m else j >= half
        place = 3 * half + j if m else j - half

        def keep(at, x):
            @pl.when(keeps)
            def _():
                nperm[place, at : at + x.shape[0], :] = x.astype(BF16)

        return (lambda: src[pl.ds(pl.multiple_of(j * size, size), size), :]), slot, keep

    copies[0].wait()
    copies[1].wait()
    for n in range(half):
        for src, base in ((before_s, 0), (after_s, 3 * half)):
            at = own * size + 5 * rows * n
            planes = [src[at + rows * i : at + rows * (i + 1), :].astype(F32) for i in range(5)]
            seen[base + n] = planes[0].astype(jnp.int32)
            which[base + n] = planes[1].astype(jnp.int32)
            value[base + n] = planes[2] + (planes[3] + planes[4])
    reorder_frames(dims, units, c_in, perm, wide, jobs, own)
    for copy in copies[2:early]:
        copy.wait()

    def where(i):
        gap = inner if i >= 2 * half else 0
        return i, i + gap, i + gap, i + gap

    arrived = [0]

    def need(i):
        last = min(max(where(i)[1] + span - own, 0), frames)
        while arrived[0] < last:
            copies[early + arrived[0]].wait()
            arrived[0] += 1

    forward_frames(
        dims, units, weight, b2s, w1, w2, w2t, wide, nperm, value, seen, which, (deriv0, deriv1), (part0, part1),
        acts, mis, grads, rest, 4 * half, where, need, lambda i: None, 0,
    )
    for copy in copies[wides:]:
        copy.wait()
    leaving = []

    def done(p):
        at = len(copies) + len(leaving)
        leaving.append(
            Copy(
                lambda: pltpu.make_async_copy(
                    result.at[pl.ds(2 * p, 2)], out.at[pl.ds(2 * p, 2)], sems.at[at]
                )
            )
        )
        leaving[-1].start()

    backward_frames(dims, units, c_in * weight, wt1, grads, qs, rest, stage, result, half, done)
    for copy in leaving:
        copy.wait()


def per_device(noisy, observed, obs_mask, obs_channel, step_index, w_first, b_first, w_second, b_second):
    frames, chans, rows, cols = noisy.shape
    hid = w_first.shape[0]
    span = w_first.shape[1] // chans
    half = span // 2
    size = chans * rows
    inner = frames - 2 * half
    count = lax.axis_size("tm")
    up = [(i, i + 1) for i in range(count - 1)]
    down = [(i + 1, i) for i in range(count - 1)]

    depth = -(-span * 9 * chans // 256) * 256
    dims = (frames, chans, rows, cols, hid, span)
    vmem = pl.BlockSpec(memory_space=pltpu.VMEM)
    smem = pl.BlockSpec(memory_space=pltpu.SMEM)
    hbm = pl.BlockSpec(memory_space=pl.ANY)
    shape = jax.ShapeDtypeStruct

    flat = noisy.reshape(frames, size, cols)
    planes = 2 * half * size + 5 * half * rows
    to_up, to_down = pl.pallas_call(
        functools.partial(pack_kernel, dims),
        out_shape=(shape((planes, cols), BF16), shape((planes, cols), BF16)),
        in_specs=[hbm] * 4,
        out_specs=(hbm, hbm),
        scratch_shapes=[
            pltpu.VMEM((2, planes, cols), BF16),
            pltpu.VMEM((2, half, rows, cols), F32),
            pltpu.VMEM((2, half, rows, cols), jnp.int32),
            pltpu.VMEM((2, half, rows, cols), jnp.int32),
            pltpu.SemaphoreType.DMA((8 + 4 * half,)),
        ],
        compiler_params=pltpu.CompilerParams(vmem_limit_bytes=62 << 20),
    )(flat, observed, obs_mask, obs_channel)
    before = pltpu.with_memory_space_constraint(lax.ppermute(to_up, "tm", up), pltpu.HBM)
    after = pltpu.with_memory_space_constraint(lax.ppermute(to_down, "tm", down), pltpu.HBM)

    wf = jnp.transpose(w_first, (2, 3, 1, 0)).reshape(9 * span * chans, hid)
    ws = jnp.transpose(w_second, (2, 3, 0, 1)).reshape(9 * chans, hid)
    weights = [
        ((hid, depth), BF16),
        ((12 * chans, 2 * hid), BF16),
        ((2 * hid, 2 * hid), BF16),
        ((18 * chans, (span + 1) * hid), BF16),
    ]
    wide_rows = (rows + 2) * 3 * chans
    work = [
        pltpu.VMEM((rows, hid, cols), F32),
        pltpu.VMEM((rows, hid, cols), F32),
        pltpu.VMEM((rows // 2, 12 * chans, cols), F32),
        pltpu.VMEM((rows // 2, 12 * chans, cols), F32),
        pltpu.VMEM((2, 2 * hid, cols), BF16),
        pltpu.VMEM((2, wide_rows + 2 * hid, cols), BF16),
    ]
    kept = [
        ((frames, wide_rows, cols), BF16),
        ((frames, size, cols), BF16),
        ((inner, rows, hid, cols), BF16),
        ((inner, size, cols), F32),
    ]
    flops = 2 * 9 * rows * cols * hid * chans * (span + 2) * inner
    results = pl.pallas_call(
        functools.partial(inner_kernel, dims),
        out_shape=tuple(shape(*k) for k in kept + weights),
        in_specs=[smem, smem] + [hbm] * 4 + [vmem] * 3,
        out_specs=(hbm,) * 8,
        scratch_shapes=[pltpu.VMEM(*w) for w in weights]
        + [pltpu.VMEM((size, size), BF16), pltpu.VMEM(*kept[0]), pltpu.VMEM(*kept[1])]
        + [pltpu.VMEM((frames, size, cols), BF16)]
        + [pltpu.VMEM((inner, rows, cols), t) for t in (F32, jnp.int32, jnp.int32)]
        + work
        + [pltpu.VMEM(*kept[2]), pltpu.VMEM(*kept[3]), pltpu.SemaphoreType.DMA((frames // 2 + 9 + 2 * inner,))],
        compiler_params=pltpu.CompilerParams(vmem_limit_bytes=62 << 20),
        cost_estimate=pl.CostEstimate(flops=4 * flops, bytes_accessed=12 << 20, transcendentals=0),
    )(step_index, b_second, flat, observed, obs_mask, obs_channel, wf, b_first.reshape(1, hid), ws)

    out = pl.pallas_call(
        functools.partial(outer_kernel, dims),
        out_shape=shape((frames, size, cols), F32),
        in_specs=[smem, smem] + [hbm] * 13,
        out_specs=hbm,
        scratch_shapes=[pltpu.VMEM(*w) for w in weights]
        + [
            pltpu.VMEM((size, size), BF16),
            pltpu.VMEM((frames + 4 * half, wide_rows, cols), BF16),
            pltpu.VMEM((4 * half, size, cols), BF16),
            pltpu.VMEM((planes, cols), BF16),
            pltpu.VMEM((planes, cols), BF16),
            pltpu.VMEM((4 * half, rows, cols), jnp.int32),
            pltpu.VMEM((4 * half, rows, cols), jnp.int32),
            pltpu.VMEM((4 * half, rows, cols), F32),
        ]
        + work
        + [
            pltpu.VMEM((frames + 2 * half, rows, hid, cols), BF16),
            pltpu.VMEM((frames + 2 * half, size, cols), F32),
            pltpu.VMEM((2, rows, 18 * chans, cols), F32),
            pltpu.VMEM((2, 2, cols // 128, size, 128), F32),
            pltpu.VMEM((frames, size, cols), F32),
            pltpu.SemaphoreType.DMA((16 + frames + frames // 2,)),
        ],
        compiler_params=pltpu.CompilerParams(vmem_limit_bytes=62 << 20),
    )(step_index, b_second, observed, obs_mask, obs_channel, before, after, *results)
    return out.reshape(frames, chans, rows, cols)


def solution(mesh):
    return jax.shard_map(
        per_device,
        mesh=mesh,
        in_specs=(
            P(("groups", "tm"), None, None, None),
            P(("groups", "tm"), None, None),
            P(("groups", "tm"), None, None),
            P(("groups", "tm"), None, None),
            P("groups"),
            P(),
            P(),
            P(),
            P(),
        ),
        out_specs=P(("groups", "tm"), None, None, None),
        check_vma=False,
    )
```

```python
import functools

import jax
import jax.numpy as jnp
import numpy as np
from jax import lax
from jax.experimental import pallas as pl
from jax.experimental.pallas import tpu as pltpu
from jax.sharding import PartitionSpec as P

STEPS = 64
sigma_low = 0.1
sigma_ratio = 20.0
F32 = jnp.float32
BF16 = jnp.bfloat16
CHUNK = 32


def shifted(x, by):
    tiles = [x[:, at : at + 128] for at in range(0, x.shape[1], 128)]
    lane = lax.broadcasted_iota(jnp.int32, tiles[0].shape, 1)
    edge = lane == (0 if by > 0 else 127)
    turned = [pltpu.roll(tile, by % 128, 1) for tile in tiles]
    beyond = [0.0] + turned[:-1] if by > 0 else turned[1:] + [0.0]
    return jnp.concatenate([jnp.where(edge, b, t) for b, t in zip(beyond, turned)], axis=1)


def sums_for(unit, size, cols, n, copies=2):
    return [[pltpu.ACC(unit)((size, cols), F32) for _ in range(n)] for _ in range(copies)]


def level_rows(step, cols):
    level = jnp.full((1, cols), step, jnp.int32).astype(F32) / F32(STEPS - 1)
    sigma = F32(sigma_low) * jnp.exp(F32(np.log(sigma_ratio)) * level)
    square = 1.0 + sigma * sigma
    return 1.0 / jnp.sqrt(square), 1.0 / square


class Copy:

    def __init__(self, make):
        self.make = make

    def start(self):
        self.make().start()

    def wait(self):
        self.make().wait()


class Unit:

    def __init__(self, index):
        self.index = index
        self.turn = 0

    def steps(self, sums, left, right):
        slot = self.turn
        self.turn = 1 - slot
        work = [lambda: pltpu.matmul_push_rhs(right(), slot, self.index)]
        at = 0
        for n, total in enumerate(sums):
            size = total.shape[0]

            def add(total=total, at=at, size=size, first=n == 0):
                pltpu.matmul_acc_lhs(
                    total, left[at : at + size, :], load_staged_rhs=slot if first else None
                )

            work.append(add)
            at += size
        return work

    def product(self, sums, left, right):
        for piece in self.steps(sums, left, lambda: right):
            piece()


def weave(*lists):
    keyed = []
    for which, pieces in enumerate(lists):
        for n, piece in enumerate(pieces):
            keyed.append(((n + 0.5) / len(pieces), which, n, piece))
    for entry in sorted(keyed, key=lambda e: e[:3]):
        entry[3]()


def build_weights(dims, wf, b1, ws, w1, w2, w2t, wt1):
    frames, chans, rows, cols, hid, span = dims
    half = span // 2
    taps = 9 * chans
    group = 3 * chans

    def first_block(k, ab):
        at = (ab * span + k) * chans
        return wf[at : at + chans, :]

    blocks = [first_block(k, ab) for k in range(span) for ab in range(9)]
    bias = b1[...]
    high = bias.astype(BF16)
    left = bias - high.astype(F32)
    mid = left.astype(BF16)
    low = (left - mid.astype(F32)).astype(BF16)
    depth = w1.shape[1]
    tail = depth - span * taps
    sub = lax.broadcasted_iota(jnp.int32, (tail, hid), 0)
    extra = jnp.where(
        sub == 0,
        high.astype(F32),
        jnp.where(sub == 1, mid.astype(F32), jnp.where(sub == 2, low.astype(F32), 0.0)),
    )
    blocks.append(extra.astype(BF16))
    stacked = jnp.concatenate(blocks, axis=0).astype(F32) * 0.5
    w1[...] = stacked.T.astype(BF16)
    second = ws[...]
    zero_group = jnp.zeros((group, hid), BF16)

    def second_block(a):
        return second[a * group : (a + 1) * group, :] if 0 <= a < 3 else zero_group

    for o in range(4):
        for i in range(2):
            w2[o * group : (o + 1) * group, i * hid : (i + 1) * hid] = second_block(i + 2 - o)
    for i in range(2):
        tall = [second_block(i + 2 - m) for m in range(4)]
        tall.append(jnp.zeros((2 * hid - 4 * group, hid), BF16))
        tall = jnp.concatenate(tall, axis=0).astype(F32) * 0.5
        w2t[i * hid : (i + 1) * hid, :] = tall.T.astype(BF16)
    for sp in range(2):
        for ab in range(9):
            for tp in range(span + 1):
                k = sp - tp + 2 * half
                at = (sp * 9 + ab) * chans
                piece = first_block(k, ab) if 0 <= k < span else jnp.zeros((chans, hid), BF16)
                wt1[at : at + chans, tp * hid : (tp + 1) * hid] = piece


def reorder_frames(dims, units, c_in, perm, wide, jobs, loops):
    frames, chans, rows, cols, hid, span = dims
    group = 3 * chans
    size = chans * rows
    i0 = lax.broadcasted_iota(jnp.int32, (size, size), 0)
    i1 = lax.broadcasted_iota(jnp.int32, (size, size), 1)
    perm[...] = jnp.where((i0 % chans) * rows + i0 // chans == i1, 1.0, 0.0).astype(BF16)
    zero = jnp.zeros((group, cols), BF16)

    def spread(x, slot, y0):
        scaled = (c_in * x).astype(BF16).astype(F32)
        shifts = [shifted(scaled, 1).astype(BF16), scaled.astype(BF16), shifted(scaled, -1).astype(BF16)]
        for y in range(x.shape[0] // chans):
            for b in range(3):
                at = (y0 + y + 1) * group + b * chans
                wide[slot, at : at + chans, :] = shifts[b][y * chans : (y + 1) * chans, :]

    def run(totals):
        for n in range(loops + 1):
            if n < loops:
                for m in range(2):
                    source, slot, keep = jobs(n, m)
                    units[m].product(totals[m][n % 2], perm, source())
                    wide[slot, 0:group, :] = zero
                    wide[slot, (rows + 1) * group :, :] = zero
            if n > 0:
                for m in range(2):
                    source, slot, keep = jobs(n - 1, m)
                    at = 0
                    for total in totals[m][(n - 1) % 2]:
                        x = pltpu.matmul_pop(total)
                        keep(at, x)
                        spread(x, slot, at // chans)
                        at += x.shape[0]

    pl.run_scoped(run, [sums_for(m, size // 4, cols, 4) for m in range(2)])


def forward_frames(
    dims, units, weight, b2s, w1, w2, w2t, wide, nperm, obs, mask, chan, deriv, part, acts, mis, grads, rest, count, where,
    need, done, noisy0,
):
    frames, chans, rows, cols, hid, span = dims
    group = 3 * chans
    pairs = rows // 2
    depth = w1.shape[1]
    tail = depth - span * 9 * chans
    sub = lax.broadcasted_iota(jnp.int32, (tail, cols), 0)
    ones = jnp.where(sub < 3, 1.0, 0.0).astype(BF16)
    row_c = lax.broadcasted_iota(jnp.int32, (chans, cols), 0)
    b2 = jnp.zeros((chans, cols), F32)
    for c in range(chans):
        b2 = jnp.where(row_c == c, b2s[c], b2)
    mis[...] = jnp.zeros(mis.shape, BF16)

    def forward(sums1, sums2, sums3):

        def issue_first(f, t):
            work = []
            for k in range(depth // cols):
                for m in range(2):
                    r = 2 * t + m

                    def right(k=k, r=r):
                        pieces = [wide[where(f)[1] + b, r * group : (r + 3) * group, :] for b in range(span)]
                        v = jnp.concatenate(pieces + [ones], axis=0)
                        return v[k * 256 : (k + 1) * 256, :]

                    work.append(units[m].steps(sums1[m][t % 2], w1.at[:, k * 256 : (k + 1) * 256], right))
            return [piece for a, b in zip(work[0::2], work[1::2]) for both in zip(a, b) for piece in both]

        def activate(t, save):
            work = []
            for m in range(2):
                at = 0
                for total in sums1[m][t % 2]:

                    def piece(m=m, at=at, total=total):
                        h = pltpu.matmul_pop(total)
                        th = jnp.tanh(h)
                        u = 1.0 + th
                        act = h * u
                        deriv[save][2 * t + m, at : at + h.shape[0], :] = u + act * (1.0 - th)
                        acts[t % 2, m * hid + at : m * hid + at + h.shape[0], :] = act.astype(BF16)

                    work.append(piece)
                    at += total.shape[0]
            return work

        def issue_second(t):
            return units[0].steps(sums2[t % 2], w2, lambda: acts[t % 2])

        def keep_second(t, save):
            def piece(o):
                part[save][t, o * group : (o + 1) * group, :] = pltpu.matmul_pop(sums2[t % 2][o])

            return [functools.partial(piece, o) for o in range(4)]

        def misfit_row(g, y, load):
            t, i = y // 2, y % 2
            total = part[load][t, (1 + i) * group : (2 + i) * group, :]
            other, o = (t + 1, 0) if i else (t - 1, 3)
            if 0 <= other < pairs:
                total = total + part[load][other, o * group : (o + 1) * group, :]
            conv = shifted(total[:chans], 1) + total[chans : 2 * chans] + shifted(total[2 * chans :], -1)
            den = nperm[noisy0 + where(g)[0], y * chans : (y + 1) * chans, :].astype(F32) + conv + b2
            seen = mask[where(g)[0], y : y + 1, :]
            code = jnp.where(seen == 1, chan[where(g)[0], y : y + 1, :], -1)
            miss = jnp.where(row_c == code, den - obs[where(g)[0], y : y + 1, :], 0.0)
            rest[where(g)[3], y * chans : (y + 1) * chans, :] = den - weight * miss
            at = (y + 1) * group
            mis[g % 2, at : at + chans, :] = shifted(miss, -1).astype(BF16)
            mis[g % 2, at + chans : at + 2 * chans, :] = miss.astype(BF16)
            mis[g % 2, at + 2 * chans : at + 3 * chans, :] = shifted(miss, 1).astype(BF16)

        def issue_third(g, q):
            at = 2 * q * group
            return units[1].steps(sums3[q % 2], w2t, lambda: mis[g % 2, at : at + 2 * hid, :])

        def keep_third(g, q, load):
            work = []
            at = 0
            for total in sums3[q % 2]:

                def piece(at=at, total=total):
                    n = total.shape[0]
                    i, low = at // hid, at % hid
                    y = 2 * q + i
                    d = pltpu.matmul_pop(total) * deriv[load][y, low : low + n, :]
                    grads[where(g)[2], y, low : low + n, :] = d.astype(BF16)

                work.append(piece)
                at += total.shape[0]
            return work

        total = count * pairs
        lag = 6
        for n in range(total + lag + 2):
            first, small, vector = [], [], []
            if 2 <= n < total + 2:
                small += issue_second((n - 2) % pairs)
            q = n - lag - 1
            if 0 <= q < total:
                small += issue_third(q // pairs, q % pairs)
            if n < total:
                if n % pairs == 0:
                    need(n // pairs)
                first += issue_first(n // pairs, n % pairs)
            if 1 <= n < total + 1:
                vector.append(activate((n - 1) % pairs, (n - 1) // pairs % 2))
            if 3 <= n < total + 3:
                vector.append(keep_second((n - 3) % pairs, (n - 3) // pairs % 2))
            q = n - lag + 1
            if 0 <= q < total:
                g, t = q // pairs, q % pairs
                ys = ([2 * t - 1] if t else []) + [2 * t] + ([rows - 1] if t == pairs - 1 else [])
                vector.append([functools.partial(misfit_row, g, y, g % 2) for y in ys])
            q = n - lag - 2
            if q >= 0:
                vector.append(keep_third(q // pairs, q % pairs, q // pairs % 2))
            weave(small + first, *vector)
            if q >= 0 and q % pairs == pairs - 1:
                done(q // pairs)

    pl.run_scoped(
        forward,
        [sums_for(m, CHUNK, cols, hid // CHUNK) for m in range(2)],
        sums_for(0, group, cols, 4),
        sums_for(1, CHUNK, cols, 2 * hid // CHUNK),
    )


def backward_frames(dims, units, scale, wt1, grads, qs, rest, stage, out, first, done):
    frames, chans, rows, cols, hid, span = dims
    group = 3 * chans
    pairs = rows // 2

    def put(p, sp, y, value):
        for j in range(cols // 128):
            stage[p % 2, sp, j, pl.ds(y, chans, stride=rows), :] = value[:, j * 128 : (j + 1) * 128]

    def issue(totals, p, t):
        work = []
        for k in range((span + 1) // 2):
            for m in range(2):

                def right(r=2 * t + m, slot=2 * p + 2 * k):
                    return jnp.concatenate([grads[slot, r], grads[slot + 1, r]], axis=0)

                work.append(units[m].steps(totals[m][t % 2], wt1.at[:, k * 256 : (k + 1) * 256], right))
        return [piece for a, b in zip(work[0::2], work[1::2]) for both in zip(a, b) for piece in both]

    def keep(totals, p, t):
        work = []
        for m in range(2):
            at = 0
            for total in totals[m][t % 2]:

                def piece(m=m, at=at, total=total):
                    qs[p % 2, 2 * t + m, at : at + total.shape[0], :] = pltpu.matmul_pop(total)

                work.append(piece)
                at += total.shape[0]
        return work

    def out_row(p, y, sp):
        total = None
        for a in range(3):
            r = y - a + 1
            if 0 <= r < rows:
                at = (sp * 3 + a) * group
                term = qs[p % 2, r, at : at + group, :]
                total = term if total is None else total + term
        back = shifted(total[:chans], -1) + total[chans : 2 * chans] + shifted(total[2 * chans :], 1)
        own = rest[first + 2 * p + sp, y * chans : (y + 1) * chans, :]
        put(p, sp, y, own - scale * back)

    def store(p):
        for sp in range(2):
            for j in range(cols // 128):
                out[2 * p + sp, :, j * 128 : (j + 1) * 128] = stage[p % 2, sp, j]

    def backward(totals):
        steps = frames // 2 * pairs
        for n in range(steps + 2):
            lists = []
            if n < steps:
                lists.append(issue(totals, n // pairs, n % pairs))
            q = n - 1
            if 0 <= q < steps:
                lists.append(keep(totals, q // pairs, q % pairs))
            q = n - 2
            if q >= 0:
                p, t = q // pairs, q % pairs
                ys = ([2 * t - 1] if t else []) + [2 * t] + ([rows - 1] if t == pairs - 1 else [])
                lists.append([functools.partial(out_row, p, y, sp) for y in ys for sp in range(2)])
            weave(*lists)
            if q >= 0 and t == pairs - 1:
                store(p)
                done(p)

    pl.run_scoped(backward, [sums_for(m, group, cols, 6) for m in range(2)])


def pack_kernel(dims, noisy, obs, mask, chan, up, down, obs_s, mask_s, chan_s, sems):
    frames, chans, rows, cols, hid, span = dims
    half = span // 2
    size = chans * rows
    own = 2 * half
    ends = ((up, frames - own, frames - half), (down, 0, 0))
    copies = []

    def copy(src, dst, n):
        copies.append(pltpu.make_async_copy(src, dst, sems.at[n]))
        copies[-1].start()

    for d, (to, first, frame0) in enumerate(ends):
        for n, (src, dst) in enumerate(((obs, obs_s), (mask, mask_s), (chan, chan_s))):
            copy(src.at[pl.ds(frame0, half)], dst.at[d], 4 * d + n)
    for d, (to, first, frame0) in enumerate(ends):
        for n in range(own):
            copy(noisy.at[first + n], to.at[pl.ds(n * size, size)], 8 + own * d + n)
    for c in copies[:6]:
        c.wait()
    for d in range(2):
        at = own * size
        for n in range(half):
            seen = mask_s[d, n].astype(F32).astype(BF16)
            which = chan_s[d, n].astype(F32).astype(BF16)
            value = obs_s[d, n]
            high = value.astype(BF16)
            left = value - high.astype(F32)
            mid = left.astype(BF16)
            low = (left - mid.astype(F32)).astype(BF16)
            for plane in (seen, which, high, mid, low):
                ends[d][0][at : at + rows, :] = plane
                at += rows
    for c in copies[6:]:
        c.wait()


def inner_kernel(
    dims, step, b2s, noisy, obs, mask, chan, wf, b1, ws,
    wide_out, nperm_out, grads_out, rest_out, w1_out, w2_out, w2t_out, wt1_out,
    w1, w2, w2t, wt1, perm, wide, nperm, noisy_s, obs_s, mask_s, chan_s, deriv0, deriv1, part0, part1, acts, mis,
    grads, rest, sems,
):
    frames, chans, rows, cols, hid, span = dims
    half = span // 2
    inner = frames - 2 * half
    units = (Unit(0), Unit(1))
    c_in, weight = level_rows(step[0], cols)
    arriving = [
        Copy(
            lambda n=n: pltpu.make_async_copy(
                noisy.at[pl.ds(2 * n, 2)], noisy_s.at[pl.ds(2 * n, 2)], sems.at[n]
            )
        )
        for n in range(frames // 2)
    ]
    for a, b in ((obs, obs_s), (mask, mask_s), (chan, chan_s)):
        at = len(arriving)
        arriving.append(
            Copy(lambda a=a, b=b, at=at: pltpu.make_async_copy(a.at[pl.ds(half, inner)], b, sems.at[at]))
        )
    for c in arriving:
        c.start()
    copies = []

    def leave(a, b, i=None):
        at = len(arriving) + len(copies)

        def make():
            if i is None:
                return pltpu.make_async_copy(a, b, sems.at[at])
            return pltpu.make_async_copy(a.at[i], b.at[i], sems.at[at])

        copies.append(Copy(make))
        copies[-1].start()

    build_weights(dims, wf, b1, ws, w1, w2, w2t, wt1)
    for a, b in ((w1, w1_out), (w2, w2_out), (w2t, w2t_out), (wt1, wt1_out)):
        leave(a, b)

    def jobs(j, m):
        f = 2 * j + m

        def keep(at, x):
            nperm[f, at : at + x.shape[0], :] = x.astype(BF16)

        def source():
            if m == 0:
                arriving[j].wait()
            return noisy_s[f]

        return source, f, keep

    reorder_frames(dims, units, c_in, perm, wide, jobs, frames // 2)
    leave(wide, wide_out)
    leave(nperm, nperm_out)
    for c in arriving[frames // 2 :]:
        c.wait()

    def done(i):
        leave(grads, grads_out, i)
        leave(rest, rest_out, i)

    forward_frames(
        dims, units, weight, b2s, w1, w2, w2t, wide, nperm, obs_s, mask_s, chan_s, (deriv0, deriv1), (part0, part1),
        acts, mis, grads, rest, inner, lambda i: (i, i, i, i), lambda i: None, done, half,
    )
    for copy in copies:
        copy.wait()


def outer_kernel(
    dims, step, b2s, obs, mask, chan, before_s, after_s,
    wide_in, nperm_in, grads_in, rest_in, w1_in, w2_in, w2t_in, wt1_in,
    out,
    w1, w2, w2t, wt1, perm, wide, nperm, seen, which, value, deriv0, deriv1, part0, part1, acts, mis,
    grads, rest, qs, stage, result, sems,
):
    frames, chans, rows, cols, hid, span = dims
    half = span // 2
    size = chans * rows
    own = 2 * half
    units = (Unit(0), Unit(1))
    inner = frames - 2 * half
    c_in, weight = level_rows(step[0], cols)
    copies = []

    def arrive(a, b, from_at=None, to_at=None, count=None):
        n = len(copies)

        def make():
            src = a if from_at is None else a.at[pl.ds(from_at, count)]
            dst = b if to_at is None else b.at[pl.ds(to_at, count)]
            return pltpu.make_async_copy(src, dst, sems.at[n])

        copies.append(Copy(make))
        copies[-1].start()

    for a, b in ((mask, seen), (chan, which), (obs, value)):
        arrive(a, b, 0, half, half)
        arrive(a, b, frames - half, 2 * half, half)
    for a, b in ((w1_in, w1), (w2_in, w2), (w2t_in, w2t)):
        arrive(a, b)
    arrive(nperm_in, nperm, 0, half, half)
    arrive(nperm_in, nperm, frames - half, 2 * half, half)
    early = len(copies)
    for n in range(frames):
        arrive(wide_in, wide, n, own + n, 1)
    wides = len(copies)
    arrive(wt1_in, wt1)
    arrive(grads_in, grads, 0, 2 * half, inner)
    arrive(rest_in, rest, 0, 2 * half, inner)

    def jobs(j, m):
        src = after_s if m else before_s
        slot = own + frames + j if m else j
        keeps = j < half if m else j >= half
        place = 3 * half + j if m else j - half

        def keep(at, x):
            if keeps:
                nperm[place, at : at + x.shape[0], :] = x.astype(BF16)

        return (lambda: src[j * size : (j + 1) * size, :]), slot, keep

    for n in range(half):
        for src, base in ((before_s, 0), (after_s, 3 * half)):
            at = own * size + 5 * rows * n
            planes = [src[at + rows * i : at + rows * (i + 1), :].astype(F32) for i in range(5)]
            seen[base + n] = planes[0].astype(jnp.int32)
            which[base + n] = planes[1].astype(jnp.int32)
            value[base + n] = planes[2] + (planes[3] + planes[4])
    reorder_frames(dims, units, c_in, perm, wide, jobs, own)
    for copy in copies[:early]:
        copy.wait()

    def where(i):
        gap = inner if i >= 2 * half else 0
        return i, i + gap, i + gap, i + gap

    arrived = [0]

    def need(i):
        last = min(max(where(i)[1] + span - own, 0), frames)
        while arrived[0] < last:
            copies[early + arrived[0]].wait()
            arrived[0] += 1

    forward_frames(
        dims, units, weight, b2s, w1, w2, w2t, wide, nperm, value, seen, which, (deriv0, deriv1), (part0, part1),
        acts, mis, grads, rest, 4 * half, where, need, lambda i: None, 0,
    )
    for copy in copies[wides:]:
        copy.wait()
    leaving = []

    def done(p):
        at = len(copies) + len(leaving)
        leaving.append(
            Copy(
                lambda: pltpu.make_async_copy(
                    result.at[pl.ds(2 * p, 2)], out.at[pl.ds(2 * p, 2)], sems.at[at]
                )
            )
        )
        leaving[-1].start()

    backward_frames(dims, units, c_in * weight, wt1, grads, qs, rest, stage, result, half, done)
    for copy in leaving:
        copy.wait()


def per_device(noisy, observed, obs_mask, obs_channel, step_index, w_first, b_first, w_second, b_second):
    frames, chans, rows, cols = noisy.shape
    hid = w_first.shape[0]
    span = w_first.shape[1] // chans
    half = span // 2
    size = chans * rows
    inner = frames - 2 * half
    count = lax.axis_size("tm")
    up = [(i, i + 1) for i in range(count - 1)]
    down = [(i + 1, i) for i in range(count - 1)]

    depth = -(-span * 9 * chans // 256) * 256
    dims = (frames, chans, rows, cols, hid, span)
    vmem = pl.BlockSpec(memory_space=pltpu.VMEM)
    smem = pl.BlockSpec(memory_space=pltpu.SMEM)
    hbm = pl.BlockSpec(memory_space=pl.ANY)
    shape = jax.ShapeDtypeStruct

    flat = noisy.reshape(frames, size, cols)
    planes = 2 * half * size + 5 * half * rows
    to_up, to_down = pl.pallas_call(
        functools.partial(pack_kernel, dims),
        out_shape=(pltpu.VMEM((planes, cols), BF16), pltpu.VMEM((planes, cols), BF16)),
        in_specs=[hbm] * 4,
        out_specs=(vmem, vmem),
        scratch_shapes=[
            pltpu.VMEM((2, half, rows, cols), F32),
            pltpu.VMEM((2, half, rows, cols), jnp.int32),
            pltpu.VMEM((2, half, rows, cols), jnp.int32),
            pltpu.SemaphoreType.DMA((8 + 4 * half,)),
        ],
    )(flat, observed, obs_mask, obs_channel)
    before = pltpu.with_memory_space_constraint(lax.ppermute(to_up, "tm", up), pltpu.VMEM)
    after = pltpu.with_memory_space_constraint(lax.ppermute(to_down, "tm", down), pltpu.VMEM)

    wf = jnp.transpose(w_first, (2, 3, 1, 0)).reshape(9 * span * chans, hid)
    ws = jnp.transpose(w_second, (2, 3, 0, 1)).reshape(9 * chans, hid)
    weights = [
        ((hid, depth), BF16),
        ((12 * chans, 2 * hid), BF16),
        ((2 * hid, 2 * hid), BF16),
        ((18 * chans, (span + 1) * hid), BF16),
    ]
    wide_rows = (rows + 2) * 3 * chans
    work = [
        pltpu.VMEM((rows, hid, cols), F32),
        pltpu.VMEM((rows, hid, cols), F32),
        pltpu.VMEM((rows // 2, 12 * chans, cols), F32),
        pltpu.VMEM((rows // 2, 12 * chans, cols), F32),
        pltpu.VMEM((2, 2 * hid, cols), BF16),
        pltpu.VMEM((2, wide_rows + 2 * hid, cols), BF16),
    ]
    kept = [
        ((frames, wide_rows, cols), BF16),
        ((frames, size, cols), BF16),
        ((inner, rows, hid, cols), BF16),
        ((inner, size, cols), F32),
    ]
    flops = 2 * 9 * rows * cols * hid * chans * (span + 2) * inner
    results = pl.pallas_call(
        functools.partial(inner_kernel, dims),
        out_shape=tuple(shape(*k) for k in kept + weights),
        in_specs=[smem, smem] + [hbm] * 4 + [vmem] * 3,
        out_specs=(hbm,) * 8,
        scratch_shapes=[pltpu.VMEM(*w) for w in weights]
        + [pltpu.VMEM((size, size), BF16), pltpu.VMEM(*kept[0]), pltpu.VMEM(*kept[1])]
        + [pltpu.VMEM((frames, size, cols), BF16)]
        + [pltpu.VMEM((inner, rows, cols), t) for t in (F32, jnp.int32, jnp.int32)]
        + work
        + [pltpu.VMEM(*kept[2]), pltpu.VMEM(*kept[3]), pltpu.SemaphoreType.DMA((frames // 2 + 9 + 2 * inner,))],
        compiler_params=pltpu.CompilerParams(vmem_limit_bytes=62 << 20),
        cost_estimate=pl.CostEstimate(flops=4 * flops, bytes_accessed=12 << 20, transcendentals=0),
    )(step_index, b_second, flat, observed, obs_mask, obs_channel, wf, b_first.reshape(1, hid), ws)

    out = pl.pallas_call(
        functools.partial(outer_kernel, dims),
        out_shape=shape((frames, size, cols), F32),
        in_specs=[smem, smem] + [hbm] * 3 + [vmem] * 2 + [hbm] * 8,
        out_specs=hbm,
        scratch_shapes=[pltpu.VMEM(*w) for w in weights]
        + [
            pltpu.VMEM((size, size), BF16),
            pltpu.VMEM((frames + 4 * half, wide_rows, cols), BF16),
            pltpu.VMEM((4 * half, size, cols), BF16),
            pltpu.VMEM((4 * half, rows, cols), jnp.int32),
            pltpu.VMEM((4 * half, rows, cols), jnp.int32),
            pltpu.VMEM((4 * half, rows, cols), F32),
        ]
        + work
        + [
            pltpu.VMEM((frames + 2 * half, rows, hid, cols), BF16),
            pltpu.VMEM((frames + 2 * half, size, cols), F32),
            pltpu.VMEM((2, rows, 18 * chans, cols), F32),
            pltpu.VMEM((2, 2, cols // 128, size, 128), F32),
            pltpu.VMEM((frames, size, cols), F32),
            pltpu.SemaphoreType.DMA((16 + frames + frames // 2,)),
        ],
        compiler_params=pltpu.CompilerParams(vmem_limit_bytes=56 << 20),
    )(step_index, b_second, observed, obs_mask, obs_channel, before, after, *results)
    return out.reshape(frames, chans, rows, cols)


def solution(mesh):
    return jax.shard_map(
        per_device,
        mesh=mesh,
        in_specs=(
            P(("groups", "tm"), None, None, None),
            P(("groups", "tm"), None, None),
            P(("groups", "tm"), None, None),
            P(("groups", "tm"), None, None),
            P("groups"),
            P(),
            P(),
            P(),
            P(),
        ),
        out_specs=P(("groups", "tm"), None, None, None),
        check_vma=False,
    )
```

```python
import functools

import jax
import jax.numpy as jnp
import numpy as np
from jax import lax
from jax.experimental import pallas as pl
from jax.experimental.pallas import tpu as pltpu
from jax.sharding import PartitionSpec as P

STEPS = 64
sigma_low = 0.1
sigma_ratio = 20.0
F32 = jnp.float32
BF16 = jnp.bfloat16
CHUNK = 64


def shifted(x, by):
    tiles = [x[:, at : at + 128] for at in range(0, x.shape[1], 128)]
    lane = lax.broadcasted_iota(jnp.int32, tiles[0].shape, 1)
    edge = lane == (0 if by > 0 else 127)
    turned = [pltpu.roll(tile, by % 128, 1) for tile in tiles]
    beyond = [0.0] + turned[:-1] if by > 0 else turned[1:] + [0.0]
    return jnp.concatenate([jnp.where(edge, b, t) for b, t in zip(beyond, turned)], axis=1)


def sums_for(unit, size, cols, n, copies=2):
    return [[pltpu.ACC(unit)((size, cols), F32) for _ in range(n)] for _ in range(copies)]


def level_rows(step, cols):
    level = jnp.full((1, cols), step, jnp.int32).astype(F32) / F32(STEPS - 1)
    sigma = F32(sigma_low) * jnp.exp(F32(np.log(sigma_ratio)) * level)
    square = 1.0 + sigma * sigma
    return 1.0 / jnp.sqrt(square), 1.0 / square


class Copy:

    def __init__(self, make):
        self.make = make

    def start(self):
        self.make().start()

    def wait(self):
        self.make().wait()


class Unit:

    def __init__(self, index):
        self.index = index
        self.turn = 0

    def steps(self, sums, left, right):
        slot = self.turn
        self.turn = 1 - slot
        work = [lambda: pltpu.matmul_push_rhs(right(), slot, self.index)]
        at = 0
        for n, total in enumerate(sums):
            size = total.shape[0]

            def add(total=total, at=at, size=size, first=n == 0):
                pltpu.matmul_acc_lhs(
                    total, left[at : at + size, :], load_staged_rhs=slot if first else None
                )

            work.append(add)
            at += size
        return work

    def product(self, sums, left, right):
        for piece in self.steps(sums, left, lambda: right):
            piece()


def weave(*lists):
    keyed = []
    for which, pieces in enumerate(lists):
        for n, piece in enumerate(pieces):
            keyed.append(((n + 0.5) / len(pieces), which, n, piece))
    for entry in sorted(keyed, key=lambda e: e[:3]):
        entry[3]()


def build_weights(dims, wf, b1, ws, w1, w2, w2t, wt1):
    frames, chans, rows, cols, hid, span = dims
    half = span // 2
    taps = 9 * chans
    group = 3 * chans

    def first_block(k, ab):
        at = (ab * span + k) * chans
        return wf[at : at + chans, :]

    blocks = [first_block(k, ab) for k in range(span) for ab in range(9)]
    bias = b1[...]
    high = bias.astype(BF16)
    left = bias - high.astype(F32)
    mid = left.astype(BF16)
    low = (left - mid.astype(F32)).astype(BF16)
    depth = w1.shape[1]
    tail = depth - span * taps
    sub = lax.broadcasted_iota(jnp.int32, (tail, hid), 0)
    extra = jnp.where(
        sub == 0,
        high.astype(F32),
        jnp.where(sub == 1, mid.astype(F32), jnp.where(sub == 2, low.astype(F32), 0.0)),
    )
    blocks.append(extra.astype(BF16))
    stacked = jnp.concatenate(blocks, axis=0).astype(F32) * 0.5
    w1[...] = stacked.T.astype(BF16)
    second = ws[...]
    zero_group = jnp.zeros((group, hid), BF16)

    def second_block(a):
        return second[a * group : (a + 1) * group, :] if 0 <= a < 3 else zero_group

    for o in range(4):
        for i in range(2):
            w2[o * group : (o + 1) * group, i * hid : (i + 1) * hid] = second_block(i + 2 - o)
    for i in range(2):
        tall = [second_block(i + 2 - m) for m in range(4)]
        tall.append(jnp.zeros((2 * hid - 4 * group, hid), BF16))
        tall = jnp.concatenate(tall, axis=0).astype(F32) * 0.5
        w2t[i * hid : (i + 1) * hid, :] = tall.T.astype(BF16)
    for sp in range(2):
        for ab in range(9):
            for tp in range(span + 1):
                k = sp - tp + 2 * half
                at = (sp * 9 + ab) * chans
                piece = first_block(k, ab) if 0 <= k < span else jnp.zeros((chans, hid), BF16)
                wt1[at : at + chans, tp * hid : (tp + 1) * hid] = piece


def reorder_frames(dims, units, c_in, perm, wide, jobs, loops):
    frames, chans, rows, cols, hid, span = dims
    group = 3 * chans
    size = chans * rows
    i0 = lax.broadcasted_iota(jnp.int32, (size, size), 0)
    i1 = lax.broadcasted_iota(jnp.int32, (size, size), 1)
    perm[...] = jnp.where((i0 % chans) * rows + i0 // chans == i1, 1.0, 0.0).astype(BF16)
    zero = jnp.zeros((group, cols), BF16)

    def spread(x, slot, y0):
        scaled = (c_in * x).astype(BF16).astype(F32)
        shifts = [shifted(scaled, 1).astype(BF16), scaled.astype(BF16), shifted(scaled, -1).astype(BF16)]
        for y in range(x.shape[0] // chans):
            for b in range(3):
                at = (y0 + y + 1) * group + b * chans
                wide[slot, at : at + chans, :] = shifts[b][y * chans : (y + 1) * chans, :]

    def run(totals):
        for n in range(loops + 1):
            if n < loops:
                for m in range(2):
                    source, slot, keep = jobs(n, m)
                    units[m].product(totals[m][n % 2], perm, source())
                    wide[slot, 0:group, :] = zero
                    wide[slot, (rows + 1) * group :, :] = zero
            if n > 0:
                for m in range(2):
                    source, slot, keep = jobs(n - 1, m)
                    at = 0
                    for total in totals[m][(n - 1) % 2]:
                        x = pltpu.matmul_pop(total)
                        keep(at, x)
                        spread(x, slot, at // chans)
                        at += x.shape[0]

    pl.run_scoped(run, [sums_for(m, size // 4, cols, 4) for m in range(2)])


def forward_frames(
    dims, units, weight, b2s, w1, w2, w2t, wide, nperm, obs, mask, chan, deriv, part, acts, mis, grads, rest, count, where,
    need, done, noisy0,
):
    frames, chans, rows, cols, hid, span = dims
    group = 3 * chans
    pairs = rows // 2
    depth = w1.shape[1]
    tail = depth - span * 9 * chans
    sub = lax.broadcasted_iota(jnp.int32, (tail, cols), 0)
    ones = jnp.where(sub < 3, 1.0, 0.0).astype(BF16)
    row_c = lax.broadcasted_iota(jnp.int32, (chans, cols), 0)
    b2 = jnp.zeros((chans, cols), F32)
    for c in range(chans):
        b2 = jnp.where(row_c == c, b2s[c], b2)
    mis[...] = jnp.zeros(mis.shape, BF16)

    def forward(sums1, sums2, sums3):

        def issue_first(f, t):
            work = []
            for k in range(depth // cols):
                for m in range(2):
                    r = 2 * t + m

                    def right(k=k, r=r):
                        pieces = [wide[where(f)[1] + b, r * group : (r + 3) * group, :] for b in range(span)]
                        v = jnp.concatenate(pieces + [ones], axis=0)
                        return v[k * 256 : (k + 1) * 256, :]

                    work.append(units[m].steps(sums1[m][t % 2], w1.at[:, k * 256 : (k + 1) * 256], right))
            return [piece for a, b in zip(work[0::2], work[1::2]) for both in zip(a, b) for piece in both]

        def activate(t, save):
            work = []
            for m in range(2):
                at = 0
                for total in sums1[m][t % 2]:

                    def piece(m=m, at=at, total=total):
                        h = pltpu.matmul_pop(total)
                        th = jnp.tanh(h)
                        u = 1.0 + th
                        act = h * u
                        deriv[save][2 * t + m, at : at + h.shape[0], :] = u + act * (1.0 - th)
                        acts[t % 2, m * hid + at : m * hid + at + h.shape[0], :] = act.astype(BF16)

                    work.append(piece)
                    at += total.shape[0]
            return work

        def issue_second(t):
            return units[0].steps(sums2[t % 2], w2, lambda: acts[t % 2])

        def keep_second(t, save):
            def piece(o):
                part[save][t, o * group : (o + 1) * group, :] = pltpu.matmul_pop(sums2[t % 2][o])

            return [functools.partial(piece, o) for o in range(4)]

        def misfit_row(g, y, load):
            t, i = y // 2, y % 2
            total = part[load][t, (1 + i) * group : (2 + i) * group, :]
            other, o = (t + 1, 0) if i else (t - 1, 3)
            if 0 <= other < pairs:
                total = total + part[load][other, o * group : (o + 1) * group, :]
            conv = shifted(total[:chans], 1) + total[chans : 2 * chans] + shifted(total[2 * chans :], -1)
            den = nperm[noisy0 + where(g)[0], y * chans : (y + 1) * chans, :].astype(F32) + conv + b2
            seen = mask[where(g)[0], y : y + 1, :]
            code = jnp.where(seen == 1, chan[where(g)[0], y : y + 1, :], -1)
            miss = jnp.where(row_c == code, den - obs[where(g)[0], y : y + 1, :], 0.0)
            rest[where(g)[3], y * chans : (y + 1) * chans, :] = den - weight * miss
            at = (y + 1) * group
            mis[g % 2, at : at + chans, :] = shifted(miss, -1).astype(BF16)
            mis[g % 2, at + chans : at + 2 * chans, :] = miss.astype(BF16)
            mis[g % 2, at + 2 * chans : at + 3 * chans, :] = shifted(miss, 1).astype(BF16)

        def issue_third(g, q):
            at = 2 * q * group
            return units[1].steps(sums3[q % 2], w2t, lambda: mis[g % 2, at : at + 2 * hid, :])

        def keep_third(g, q, load):
            work = []
            at = 0
            for total in sums3[q % 2]:

                def piece(at=at, total=total):
                    n = total.shape[0]
                    i, low = at // hid, at % hid
                    y = 2 * q + i
                    d = pltpu.matmul_pop(total) * deriv[load][y, low : low + n, :]
                    grads[where(g)[2], y, low : low + n, :] = d.astype(BF16)

                work.append(piece)
                at += total.shape[0]
            return work

        total = count * pairs
        lag = 6
        for n in range(total + lag + 2):
            first, small, vector = [], [], []
            if 2 <= n < total + 2:
                small += issue_second((n - 2) % pairs)
            q = n - lag - 1
            if 0 <= q < total:
                small += issue_third(q // pairs, q % pairs)
            if n < total:
                if n % pairs == 0:
                    need(n // pairs)
                first += issue_first(n // pairs, n % pairs)
            if 1 <= n < total + 1:
                vector.append(activate((n - 1) % pairs, (n - 1) // pairs % 2))
            if 3 <= n < total + 3:
                vector.append(keep_second((n - 3) % pairs, (n - 3) // pairs % 2))
            q = n - lag + 1
            if 0 <= q < total:
                g, t = q // pairs, q % pairs
                ys = ([2 * t - 1] if t else []) + [2 * t] + ([rows - 1] if t == pairs - 1 else [])
                vector.append([functools.partial(misfit_row, g, y, g % 2) for y in ys])
            q = n - lag - 2
            if q >= 0:
                vector.append(keep_third(q // pairs, q % pairs, q // pairs % 2))
            weave(small + first, *vector)
            if q >= 0 and q % pairs == pairs - 1:
                done(q // pairs)

    pl.run_scoped(
        forward,
        [sums_for(m, CHUNK, cols, hid // CHUNK) for m in range(2)],
        sums_for(0, group, cols, 4),
        sums_for(1, CHUNK, cols, 2 * hid // CHUNK),
    )


def backward_frames(dims, units, scale, wt1, grads, qs, rest, stage, out, first, done):
    frames, chans, rows, cols, hid, span = dims
    group = 3 * chans
    pairs = rows // 2

    def put(p, sp, y, value):
        for j in range(cols // 128):
            stage[p % 2, sp, j, pl.ds(y, chans, stride=rows), :] = value[:, j * 128 : (j + 1) * 128]

    def issue(totals, p, t):
        work = []
        for k in range((span + 1) // 2):
            for m in range(2):

                def right(r=2 * t + m, slot=2 * p + 2 * k):
                    return jnp.concatenate([grads[slot, r], grads[slot + 1, r]], axis=0)

                work.append(units[m].steps(totals[m][t % 2], wt1.at[:, k * 256 : (k + 1) * 256], right))
        return [piece for a, b in zip(work[0::2], work[1::2]) for both in zip(a, b) for piece in both]

    def keep(totals, p, t):
        work = []
        for m in range(2):
            at = 0
            for total in totals[m][t % 2]:

                def piece(m=m, at=at, total=total):
                    qs[p % 2, 2 * t + m, at : at + total.shape[0], :] = pltpu.matmul_pop(total)

                work.append(piece)
                at += total.shape[0]
        return work

    def out_row(p, y, sp):
        total = None
        for a in range(3):
            r = y - a + 1
            if 0 <= r < rows:
                at = (sp * 3 + a) * group
                term = qs[p % 2, r, at : at + group, :]
                total = term if total is None else total + term
        back = shifted(total[:chans], -1) + total[chans : 2 * chans] + shifted(total[2 * chans :], 1)
        own = rest[first + 2 * p + sp, y * chans : (y + 1) * chans, :]
        put(p, sp, y, own - scale * back)

    def store(p):
        for sp in range(2):
            for j in range(cols // 128):
                out[2 * p + sp, :, j * 128 : (j + 1) * 128] = stage[p % 2, sp, j]

    def backward(totals):
        steps = frames // 2 * pairs
        for n in range(steps + 2):
            lists = []
            if n < steps:
                lists.append(issue(totals, n // pairs, n % pairs))
            q = n - 1
            if 0 <= q < steps:
                lists.append(keep(totals, q // pairs, q % pairs))
            q = n - 2
            if q >= 0:
                p, t = q // pairs, q % pairs
                ys = ([2 * t - 1] if t else []) + [2 * t] + ([rows - 1] if t == pairs - 1 else [])
                lists.append([functools.partial(out_row, p, y, sp) for y in ys for sp in range(2)])
            weave(*lists)
            if q >= 0 and t == pairs - 1:
                store(p)
                done(p)

    pl.run_scoped(backward, [sums_for(m, group, cols, 6) for m in range(2)])


def pack_kernel(dims, noisy, obs, mask, chan, up, down, obs_s, mask_s, chan_s, sems):
    frames, chans, rows, cols, hid, span = dims
    half = span // 2
    size = chans * rows
    own = 2 * half
    ends = ((up, frames - own, frames - half), (down, 0, 0))
    copies = []

    def copy(src, dst, n):
        copies.append(pltpu.make_async_copy(src, dst, sems.at[n]))
        copies[-1].start()

    for d, (to, first, frame0) in enumerate(ends):
        for n, (src, dst) in enumerate(((obs, obs_s), (mask, mask_s), (chan, chan_s))):
            copy(src.at[pl.ds(frame0, half)], dst.at[d], 4 * d + n)
    for d, (to, first, frame0) in enumerate(ends):
        for n in range(own):
            copy(noisy.at[first + n], to.at[pl.ds(n * size, size)], 8 + own * d + n)
    for c in copies[:6]:
        c.wait()
    for d in range(2):
        at = own * size
        for n in range(half):
            seen = mask_s[d, n].astype(F32).astype(BF16)
            which = chan_s[d, n].astype(F32).astype(BF16)
            value = obs_s[d, n]
            high = value.astype(BF16)
            left = value - high.astype(F32)
            mid = left.astype(BF16)
            low = (left - mid.astype(F32)).astype(BF16)
            for plane in (seen, which, high, mid, low):
                ends[d][0][at : at + rows, :] = plane
                at += rows
    for c in copies[6:]:
        c.wait()


def inner_kernel(
    dims, step, b2s, noisy, obs, mask, chan, wf, b1, ws,
    wide_out, nperm_out, grads_out, rest_out, w1_out, w2_out, w2t_out, wt1_out,
    w1, w2, w2t, wt1, perm, wide, nperm, noisy_s, obs_s, mask_s, chan_s, deriv0, deriv1, part0, part1, acts, mis,
    grads, rest, sems,
):
    frames, chans, rows, cols, hid, span = dims
    half = span // 2
    inner = frames - 2 * half
    units = (Unit(0), Unit(1))
    c_in, weight = level_rows(step[0], cols)
    arriving = [
        Copy(
            lambda n=n: pltpu.make_async_copy(
                noisy.at[pl.ds(2 * n, 2)], noisy_s.at[pl.ds(2 * n, 2)], sems.at[n]
            )
        )
        for n in range(frames // 2)
    ]
    for a, b in ((obs, obs_s), (mask, mask_s), (chan, chan_s)):
        at = len(arriving)
        arriving.append(
            Copy(lambda a=a, b=b, at=at: pltpu.make_async_copy(a.at[pl.ds(half, inner)], b, sems.at[at]))
        )
    for c in arriving:
        c.start()
    copies = []

    def leave(a, b, i=None):
        at = len(arriving) + len(copies)

        def make():
            if i is None:
                return pltpu.make_async_copy(a, b, sems.at[at])
            return pltpu.make_async_copy(a.at[i], b.at[i], sems.at[at])

        copies.append(Copy(make))
        copies[-1].start()

    build_weights(dims, wf, b1, ws, w1, w2, w2t, wt1)
    for a, b in ((w1, w1_out), (w2, w2_out), (w2t, w2t_out), (wt1, wt1_out)):
        leave(a, b)

    def jobs(j, m):
        f = 2 * j + m

        def keep(at, x):
            nperm[f, at : at + x.shape[0], :] = x.astype(BF16)

        def source():
            if m == 0:
                arriving[j].wait()
            return noisy_s[f]

        return source, f, keep

    reorder_frames(dims, units, c_in, perm, wide, jobs, frames // 2)
    leave(wide, wide_out)
    leave(nperm, nperm_out)
    for c in arriving[frames // 2 :]:
        c.wait()

    def done(i):
        leave(grads, grads_out, i)
        leave(rest, rest_out, i)

    forward_frames(
        dims, units, weight, b2s, w1, w2, w2t, wide, nperm, obs_s, mask_s, chan_s, (deriv0, deriv1), (part0, part1),
        acts, mis, grads, rest, inner, lambda i: (i, i, i, i), lambda i: None, done, half,
    )
    for copy in copies:
        copy.wait()


def outer_kernel(
    dims, step, b2s, obs, mask, chan, before_s, after_s,
    wide_in, nperm_in, grads_in, rest_in, w1_in, w2_in, w2t_in, wt1_in,
    out,
    w1, w2, w2t, wt1, perm, wide, nperm, seen, which, value, deriv0, deriv1, part0, part1, acts, mis,
    grads, rest, qs, stage, result, sems,
):
    frames, chans, rows, cols, hid, span = dims
    half = span // 2
    size = chans * rows
    own = 2 * half
    units = (Unit(0), Unit(1))
    inner = frames - 2 * half
    c_in, weight = level_rows(step[0], cols)
    copies = []

    def arrive(a, b, from_at=None, to_at=None, count=None):
        n = len(copies)

        def make():
            src = a if from_at is None else a.at[pl.ds(from_at, count)]
            dst = b if to_at is None else b.at[pl.ds(to_at, count)]
            return pltpu.make_async_copy(src, dst, sems.at[n])

        copies.append(Copy(make))
        copies[-1].start()

    for a, b in ((mask, seen), (chan, which), (obs, value)):
        arrive(a, b, 0, half, half)
        arrive(a, b, frames - half, 2 * half, half)
    for a, b in ((w1_in, w1), (w2_in, w2), (w2t_in, w2t)):
        arrive(a, b)
    arrive(nperm_in, nperm, 0, half, half)
    arrive(nperm_in, nperm, frames - half, 2 * half, half)
    early = len(copies)
    for n in range(frames):
        arrive(wide_in, wide, n, own + n, 1)
    wides = len(copies)
    arrive(wt1_in, wt1)
    arrive(grads_in, grads, 0, 2 * half, inner)
    arrive(rest_in, rest, 0, 2 * half, inner)

    def jobs(j, m):
        src = after_s if m else before_s
        slot = own + frames + j if m else j
        keeps = j < half if m else j >= half
        place = 3 * half + j if m else j - half

        def keep(at, x):
            if keeps:
                nperm[place, at : at + x.shape[0], :] = x.astype(BF16)

        return (lambda: src[j * size : (j + 1) * size, :]), slot, keep

    for n in range(half):
        for src, base in ((before_s, 0), (after_s, 3 * half)):
            at = own * size + 5 * rows * n
            planes = [src[at + rows * i : at + rows * (i + 1), :].astype(F32) for i in range(5)]
            seen[base + n] = planes[0].astype(jnp.int32)
            which[base + n] = planes[1].astype(jnp.int32)
            value[base + n] = planes[2] + (planes[3] + planes[4])
    reorder_frames(dims, units, c_in, perm, wide, jobs, own)
    for copy in copies[:early]:
        copy.wait()

    def where(i):
        gap = inner if i >= 2 * half else 0
        return i, i + gap, i + gap, i + gap

    arrived = [0]

    def need(i):
        last = min(max(where(i)[1] + span - own, 0), frames)
        while arrived[0] < last:
            copies[early + arrived[0]].wait()
            arrived[0] += 1

    forward_frames(
        dims, units, weight, b2s, w1, w2, w2t, wide, nperm, value, seen, which, (deriv0, deriv1), (part0, part1),
        acts, mis, grads, rest, 4 * half, where, need, lambda i: None, 0,
    )
    for copy in copies[wides:]:
        copy.wait()
    leaving = []

    def done(p):
        at = len(copies) + len(leaving)
        leaving.append(
            Copy(
                lambda: pltpu.make_async_copy(
                    result.at[pl.ds(2 * p, 2)], out.at[pl.ds(2 * p, 2)], sems.at[at]
                )
            )
        )
        leaving[-1].start()

    backward_frames(dims, units, c_in * weight, wt1, grads, qs, rest, stage, result, half, done)
    for copy in leaving:
        copy.wait()


def per_device(noisy, observed, obs_mask, obs_channel, step_index, w_first, b_first, w_second, b_second):
    frames, chans, rows, cols = noisy.shape
    hid = w_first.shape[0]
    span = w_first.shape[1] // chans
    half = span // 2
    size = chans * rows
    inner = frames - 2 * half
    count = lax.axis_size("tm")
    up = [(i, i + 1) for i in range(count - 1)]
    down = [(i + 1, i) for i in range(count - 1)]

    depth = -(-span * 9 * chans // 256) * 256
    dims = (frames, chans, rows, cols, hid, span)
    vmem = pl.BlockSpec(memory_space=pltpu.VMEM)
    smem = pl.BlockSpec(memory_space=pltpu.SMEM)
    hbm = pl.BlockSpec(memory_space=pl.ANY)
    shape = jax.ShapeDtypeStruct

    flat = noisy.reshape(frames, size, cols)
    planes = 2 * half * size + 5 * half * rows
    to_up, to_down = pl.pallas_call(
        functools.partial(pack_kernel, dims),
        out_shape=(pltpu.VMEM((planes, cols), BF16), pltpu.VMEM((planes, cols), BF16)),
        in_specs=[hbm] * 4,
        out_specs=(vmem, vmem),
        scratch_shapes=[
            pltpu.VMEM((2, half, rows, cols), F32),
            pltpu.VMEM((2, half, rows, cols), jnp.int32),
            pltpu.VMEM((2, half, rows, cols), jnp.int32),
            pltpu.SemaphoreType.DMA((8 + 4 * half,)),
        ],
    )(flat, observed, obs_mask, obs_channel)
    before = pltpu.with_memory_space_constraint(lax.ppermute(to_up, "tm", up), pltpu.VMEM)
    after = pltpu.with_memory_space_constraint(lax.ppermute(to_down, "tm", down), pltpu.VMEM)

    wf = jnp.transpose(w_first, (2, 3, 1, 0)).reshape(9 * span * chans, hid)
    ws = jnp.transpose(w_second, (2, 3, 0, 1)).reshape(9 * chans, hid)
    weights = [
        ((hid, depth), BF16),
        ((12 * chans, 2 * hid), BF16),
        ((2 * hid, 2 * hid), BF16),
        ((18 * chans, (span + 1) * hid), BF16),
    ]
    wide_rows = (rows + 2) * 3 * chans
    work = [
        pltpu.VMEM((rows, hid, cols), F32),
        pltpu.VMEM((rows, hid, cols), F32),
        pltpu.VMEM((rows // 2, 12 * chans, cols), F32),
        pltpu.VMEM((rows // 2, 12 * chans, cols), F32),
        pltpu.VMEM((2, 2 * hid, cols), BF16),
        pltpu.VMEM((2, wide_rows + 2 * hid, cols), BF16),
    ]
    kept = [
        ((frames, wide_rows, cols), BF16),
        ((frames, size, cols), BF16),
        ((inner, rows, hid, cols), BF16),
        ((inner, size, cols), F32),
    ]
    flops = 2 * 9 * rows * cols * hid * chans * (span + 2) * inner
    results = pl.pallas_call(
        functools.partial(inner_kernel, dims),
        out_shape=tuple(shape(*k) for k in kept + weights),
        in_specs=[smem, smem] + [hbm] * 4 + [vmem] * 3,
        out_specs=(hbm,) * 8,
        scratch_shapes=[pltpu.VMEM(*w) for w in weights]
        + [pltpu.VMEM((size, size), BF16), pltpu.VMEM(*kept[0]), pltpu.VMEM(*kept[1])]
        + [pltpu.VMEM((frames, size, cols), BF16)]
        + [pltpu.VMEM((inner, rows, cols), t) for t in (F32, jnp.int32, jnp.int32)]
        + work
        + [pltpu.VMEM(*kept[2]), pltpu.VMEM(*kept[3]), pltpu.SemaphoreType.DMA((frames // 2 + 9 + 2 * inner,))],
        compiler_params=pltpu.CompilerParams(vmem_limit_bytes=62 << 20),
        cost_estimate=pl.CostEstimate(flops=4 * flops, bytes_accessed=12 << 20, transcendentals=0),
    )(step_index, b_second, flat, observed, obs_mask, obs_channel, wf, b_first.reshape(1, hid), ws)

    out = pl.pallas_call(
        functools.partial(outer_kernel, dims),
        out_shape=shape((frames, size, cols), F32),
        in_specs=[smem, smem] + [hbm] * 3 + [vmem] * 2 + [hbm] * 8,
        out_specs=hbm,
        scratch_shapes=[pltpu.VMEM(*w) for w in weights]
        + [
            pltpu.VMEM((size, size), BF16),
            pltpu.VMEM((frames + 4 * half, wide_rows, cols), BF16),
            pltpu.VMEM((4 * half, size, cols), BF16),
            pltpu.VMEM((4 * half, rows, cols), jnp.int32),
            pltpu.VMEM((4 * half, rows, cols), jnp.int32),
            pltpu.VMEM((4 * half, rows, cols), F32),
        ]
        + work
        + [
            pltpu.VMEM((frames + 2 * half, rows, hid, cols), BF16),
            pltpu.VMEM((frames + 2 * half, size, cols), F32),
            pltpu.VMEM((2, rows, 18 * chans, cols), F32),
            pltpu.VMEM((2, 2, cols // 128, size, 128), F32),
            pltpu.VMEM((frames, size, cols), F32),
            pltpu.SemaphoreType.DMA((16 + frames + frames // 2,)),
        ],
        compiler_params=pltpu.CompilerParams(vmem_limit_bytes=56 << 20),
    )(step_index, b_second, observed, obs_mask, obs_channel, before, after, *results)
    return out.reshape(frames, chans, rows, cols)


def solution(mesh):
    return jax.shard_map(
        per_device,
        mesh=mesh,
        in_specs=(
            P(("groups", "tm"), None, None, None),
            P(("groups", "tm"), None, None),
            P(("groups", "tm"), None, None),
            P(("groups", "tm"), None, None),
            P("groups"),
            P(),
            P(),
            P(),
            P(),
        ),
        out_specs=P(("groups", "tm"), None, None, None),
        check_vma=False,
    )
```
